256 devices in a mesh: chain: 32 (over x, y, core), col: 8 (over z).
Axes of the slice: x: 4, y: 4, z: 8, core: 2. Of those that a mesh axis runs over, the one named last changes fastest.
Arguments:
- rhs: bfloat16 [64, 64, 2560], P('chain', None, 'col'), may hold values from -6 to 6
- block_inverse: bfloat16 [64, 2560, 2560], P('chain', 'col'), as said below
- entry_factor: bfloat16 [64, 2560, 128], P('chain', 'col'), as said below
- exit_factor: bfloat16 [64, 2560, 128], P('chain', 'col'), as said below
- previous: bfloat16 [64, 2560], P(None, 'col'), may hold values from -6 to 6
Outputs:
- solution: float32 [64, 64, 2560], P('chain', None, 'col')
The draws below stay inside these ranges and needn't reach their ends.
Inputs may be any that keep to these rules, and one draw needn't show every extreme that they name: Every block of block_inverse equals its own transpose. `entry_factor`: entries are independent, of mean zero. `exit_factor`: entries are independent, of mean zero.
All inputs are finite; a program needn't handle non-finite values.
Results may differ from the reference program's by a relative error of at most 0.0003.
Values may be sent and summed in bfloat16 or wider, within the bound.
No kernel may reach another device: no remote copies, remote signals or barrier semaphores. Data moves between devices by JAX's collectives and lax.ppermute only.
A program may use at most 64 MiB of HBM per device.

```python
import jax
import jax.numpy as jnp
from jax import lax

B = 2560
NX = 128
COLS = 64
INTERVALS = 64


def draw_block_inverse(key, part):

    def draw_block(interval):
        subkey = jax.random.fold_in(key, interval)
        first_key, second_key = jax.random.split(subkey)
        random_part = jax.random.normal(first_key, (B, B), jnp.float32)
        symmetric = (random_part + random_part.T) * (0.6 / (2.0 * B) ** 0.5)
        diagonal_part = jax.random.uniform(second_key, (B,), jnp.float32, 0.5, 2.0)
        return (symmetric + jnp.diag(diagonal_part)).astype(jnp.bfloat16)
    return lax.map(draw_block, jnp.arange(INTERVALS))


def draw_factor(key, spread):
    shape = (INTERVALS, B, NX)
    values = jax.random.truncated_normal(key, -3.0, 3.0, shape, jnp.float32) * (spread / 0.9866)
    return values.astype(jnp.bfloat16)


def draw_entry_factor(key, part):
    return draw_factor(jax.random.fold_in(key, 11), (NX * 5.0 / 4.0) ** (-0.5))


def draw_exit_factor(key, part):
    return draw_factor(jax.random.fold_in(key, 23), (1.0 * B) ** (-0.5))


def block_scale(rng, extent, cuts, low, high):
    def one(position, parts):
        draws = jax.random.uniform(jax.random.fold_in(jax.random.fold_in(rng, 6), position), (parts,), jnp.float32, low / len(cuts), high / len(cuts))
        return jnp.repeat(jnp.exp(draws), extent[position] // parts).reshape((-1,) + (1,) * (len(extent) - position - 1))

    factor_of = one(*cuts[0])
    for cut in cuts[1:]:
        factor_of = factor_of * one(*cut)
    return factor_of


def bell_draw(key, shape, scale, reach, cuts=(), dtype=jnp.bfloat16):
    result = scale * jax.random.normal(key, shape, jnp.float32)
    if cuts:
        result = result * block_scale(key, shape, cuts, -0.22, 0.18)
    return jnp.clip(result, -reach, reach).astype(dtype)


def setup_inputs(seed: int = 0) -> dict:
    streams_of = jax.random.split(jax.random.key(seed), 6)
    rhs = bell_draw(streams_of[0], (INTERVALS, COLS, B), 1.0, 6.0, ((0, 32), (2, 8)))
    block_inverse = draw_block_inverse(jax.random.fold_in(streams_of[5], 71), 0)
    entry_factor = draw_entry_factor(jax.random.fold_in(streams_of[5], 71), 0)
    exit_factor = draw_exit_factor(jax.random.fold_in(streams_of[5], 71), 0)
    previous = bell_draw(streams_of[4], (COLS, B), 1.0, 6.0, ((1, 8),))
    return {"rhs": rhs, "block_inverse": block_inverse, "entry_factor": entry_factor, "exit_factor": exit_factor, "previous": previous}


def reference(rhs, block_inverse, entry_factor, exit_factor, previous):
    exact = lax.Precision.HIGHEST
    total_intervals = rhs.shape[0]
    carry_state = jnp.dot(previous, exit_factor[0], preferred_element_type=jnp.float32)
    applied_list = []
    couplings = []
    for interval in range(total_intervals):
        solved = rhs[interval].astype(jnp.float32) - jnp.dot(carry_state, entry_factor[interval].astype(jnp.float32).T, precision=exact)
        solved_low = solved.astype(jnp.bfloat16)
        applied_list.append(jnp.dot(solved_low, block_inverse[interval], preferred_element_type=jnp.float32))
        if interval + 1 < total_intervals:
            following = exit_factor[interval + 1]
            couple = -jnp.dot(entry_factor[interval].T, following, preferred_element_type=jnp.float32)
            source = jnp.dot(rhs[interval], following, preferred_element_type=jnp.float32)
            carry_state = jnp.dot(carry_state, couple, precision=exact) + source
            couplings.append(couple)
    behind = jnp.zeros((rhs.shape[1], entry_factor.shape[2]), jnp.float32)
    results = [None] * total_intervals
    for interval in reversed(range(total_intervals)):
        applied = applied_list[interval]
        if interval + 1 < total_intervals:
            results[interval] = applied - jnp.dot(behind, exit_factor[interval + 1].astype(jnp.float32).T, precision=exact)
        else:
            results[interval] = applied
        if interval > 0:
            carried = jnp.dot(applied.astype(jnp.bfloat16), entry_factor[interval], preferred_element_type=jnp.float32)
            if interval + 1 < total_intervals:
                behind = jnp.dot(behind, couplings[interval].T, precision=exact) + carried
            else:
                behind = carried
    return jnp.stack(results)
```

```python
import jax
import jax.numpy as jnp
from jax import lax
from jax.experimental import pallas as pl
from jax.experimental.pallas import tpu as pltpu
from jax.sharding import Mesh
from jax.sharding import PartitionSpec as P

X, Y, CORE, COL = "chain_0", "chain_1", "chain_2", "col"
CHAIN = (X, Y, CORE)
F32 = jnp.float32
BF16 = jnp.bfloat16

NN = (((1,), (0,)), ((), ()))
NT = (((1,), (1,)), ((), ()))
TN = (((0,), (0,)), ((), ()))


def dot16(a, b, dims):
    return lax.dot_general(a, b, dims, preferred_element_type=F32)


def dot32(a, b, dims):
    return lax.dot_general(a, b, dims, precision=lax.Precision.HIGHEST, preferred_element_type=F32)


def dot32_16(a, b, dims):
    high = a.astype(BF16)
    rest = a - high.astype(F32)
    middle = rest.astype(BF16)
    low = (rest - middle.astype(F32)).astype(BF16)
    rows = a.shape[0]
    out = dot16(jnp.concatenate([high, middle, low], axis=0), b, dims)
    return (out[2 * rows :] + out[rows : 2 * rows]) + out[:rows]


def vmem():
    return pl.BlockSpec(memory_space=pltpu.VMEM)


def smem():
    return pl.BlockSpec(memory_space=pltpu.SMEM)


def call(kernel, place, arrays, outs, scratch=()):
    return pl.pallas_call(
        kernel,
        out_shape=outs,
        in_specs=[smem()] + [vmem()] * len(arrays),
        out_specs=jax.tree.map(lambda _: vmem(), outs),
        scratch_shapes=list(scratch),
        compiler_params=pltpu.CompilerParams(vmem_limit_bytes=40 * 1024 * 1024),
    )(place, *arrays)


def of(shape, dtype=F32):
    return jax.ShapeDtypeStruct(shape, dtype)


def partial_kernel(place, entry, exit_, arriving, rhs, previous, out):
    groups = out.shape[0]

    def put(start, rows, value):
        out[:, start : start + rows, :] = value.reshape(groups, rows, value.shape[1])

    n = entry.shape[2] // groups
    c = rhs.shape[1] // groups
    put(0, n, -dot16(entry[0], exit_[1], TN))
    put(n, n, -dot16(entry[1], arriving[0], TN))
    put(2 * n, c, dot16(rhs[0], exit_[1], NN))
    put(2 * n + c, c, dot16(rhs[1], arriving[0], NN))
    put(2 * n + 2 * c, c, dot16(previous[...], exit_[0], NN))


def sum_kernel(place, parts, out):
    total = parts[0]
    for k in range(1, parts.shape[0]):
        total = total + parts[k]
    for k in range(parts.shape[0]):
        out[k] = total


def pieces(whole):
    groups, rows, width = whole.shape
    n = width // groups
    c = (rows - 2 * n) // 3

    def take(start, count):
        return whole[:, start : start + count, :].reshape(groups * count, width)

    return take(0, n), take(n, n), take(2 * n, c), take(2 * n + c, c), take(2 * n + 2 * c, c)


def is_first(place):
    return (place[0] == 0) & (place[1] == 0) & (place[2] == 0)


def after(earlier, later, n):
    out = dot32(earlier, later[:n], NN)
    return out[:n], out[n:] + later[n:]


def local_kernel(place, whole, out):
    couple0, couple1, source0, source1, opening = pieces(whole)
    n = couple0.shape[0]
    folded = dot32(opening, couple0, NN) + source0
    source0 = jnp.where(is_first(place), folded, source0)
    out[:n] = dot32(couple0, couple1, NN)
    out[n:] = dot32(source0, couple1, NN) + source1


def pair_kernel(place, mine, other, out, before):
    n = mine.shape[1]
    upper = place[2] == 1
    first = jnp.where(upper, other[...], mine[...])
    second = jnp.where(upper, mine[...], other[...])
    out[:n], out[n:] = after(first, second, n)
    before[...] = other[...]


def group_kernel(place, mine, one, two, three, total, before, slots):
    n = mine.shape[1]
    y = place[1]
    for d, ref in enumerate((mine, one, two, three)):
        slots[lax.rem(y - d + 4, 4)] = ref[...]
    rows = lax.broadcasted_iota(jnp.int32, mine.shape, 0)
    lanes = lax.broadcasted_iota(jnp.int32, mine.shape, 1)
    before[...] = jnp.where(rows == lanes, 1.0, 0.0).astype(F32)
    total[...] = slots[0]
    for q in range(1, 4):

        @pl.when(y == q)
        def _():
            before[...] = total[...]

        top, bottom = after(total[...], slots[q], n)
        total[:n] = top
        total[n:] = bottom


def forward_kernel(place, whole, core_other, before, one, two, three, entry, rhs, out):
    couple0, _, source0, _, opening = pieces(whole)
    n = couple0.shape[0]
    x = place[0]
    state = jnp.zeros(opening.shape, F32)
    for d, ref in ((3, three), (2, two), (1, one)):
        state = jnp.where(d <= x, dot32(state, ref[:n], NN) + ref[n:], state)
    state = dot32(state, before[:n], NN) + before[n:]
    state = jnp.where(place[2] == 1, dot32(state, core_other[:n], NN) + core_other[n:], state)
    state = jnp.where(is_first(place), opening, state)
    out[0] = (rhs[0].astype(F32) - dot32_16(state, entry[0], NT)).astype(BF16)
    state = dot32(state, couple0, NN) + source0
    out[1] = (rhs[1].astype(F32) - dot32_16(state, entry[1], NT)).astype(BF16)


def apply_kernel(place, forward, inverse, entry, applied, carried):
    groups = forward.shape[0]
    for i in range(forward.shape[1]):
        whole = jnp.concatenate([forward[g, i] for g in range(groups)], axis=1)
        value = dot16(whole, inverse[i], NT)
        applied[i] = value
        part = dot16(value.astype(BF16), entry[i], NN)
        c = part.shape[0] // groups
        carried[:, i * c : (i + 1) * c, :] = part.reshape(groups, c, part.shape[1])


def back_kernel(place, parts, whole, core_other, before, carried, send):
    couple0 = pieces(whole)[0]
    n = couple0.shape[0]
    c = parts.shape[1] // 2
    total = parts[0]
    for k in range(1, parts.shape[0]):
        total = total + parts[k]
    carried[...] = total
    x, y, core = place[0], place[1], place[2]
    own = dot32(total[c:], couple0, NT) + total[:c]
    chip = jnp.where(core == 1, dot32(own, core_other[:n], NT), own)
    group = dot32(chip, before[:n], NT)
    for k in range(send.shape[0]):
        same_x = x == k // 8
        same_y = y == (k // 2) % 4
        value = jnp.where(same_x, jnp.where(same_y, own, chip), group)
        send[k] = value


def behind_kernel(place, got, carried, whole, core_other, y1, y2, y3, x1, x2, x3, out):
    _, couple1, _, _, _ = pieces(whole)
    n = couple1.shape[0]
    c = carried.shape[0] // 2
    x, y, core = place[0], place[1], place[2]
    state = jnp.zeros((c, n), F32)
    for e, ref in ((3, x1), (2, x2), (1, x3)):
        base = lax.rem(x + e, 4) * 8
        extra = got[base]
        for k in range(1, 8):
            extra = extra + got[base + k]
        state = jnp.where(x + e <= 3, dot32(state, ref[:n], NT) + extra, state)
    for e, ref in ((3, y1), (2, y2), (1, y3)):
        base = x * 8 + lax.rem(y + e, 4) * 2
        extra = got[base] + got[base + 1]
        state = jnp.where(y + e <= 3, dot32(state, ref[:n], NT) + extra, state)
    extra = got[x * 8 + y * 2 + 1]
    state = jnp.where(core == 0, dot32(state, core_other[:n], NT) + extra, state)
    inner = dot32(state, couple1, NT) + carried[c:]
    for k in range(out.shape[0]):
        out[k, :c] = inner
        out[k, c:] = state


def final_kernel(place, got, applied, exit_, arriving, out):
    groups, rows, width = got.shape
    c = rows // 2
    inner = got[:, :c, :].reshape(groups * c, width)
    outer = got[:, c:, :].reshape(groups * c, width)
    out[0] = applied[0] - dot32_16(inner, exit_[1], NT)
    out[1] = applied[1] - dot32_16(outer, arriving[0], NT)


def exchange(value, axes):
    return lax.all_to_all(value, axes, split_axis=0, concat_axis=0, tiled=True)


def ring(value, axis):
    size = lax.axis_size(axis)
    return [
        lax.ppermute(value, axis, [(i, (i + d) % size) for i in range(size)])
        for d in range(1, size)
    ]


def shards(rhs, block_inverse, entry, exit_, previous):
    z = lax.axis_size(COL)
    here, cols, local = rhs.shape
    n = entry.shape[2]
    place = jnp.stack([lax.axis_index(X), lax.axis_index(Y), lax.axis_index(CORE)]).astype(jnp.int32)
    chain = lax.axis_size(CHAIN)
    arriving = lax.ppermute(exit_[:1], CHAIN, [(i, i - 1) for i in range(1, chain)])
    rows = (2 * n + 3 * cols) // z
    parts = call(partial_kernel, place, (entry, exit_, arriving, rhs, previous), of((z, rows, n)))
    summed = call(sum_kernel, place, (exchange(parts, COL),), of((z, rows, n)))
    whole = exchange(summed, COL)
    maps = of((n + cols, n))
    mine = call(local_kernel, place, (whole,), maps)
    other = lax.ppermute(mine, CORE, [(0, 1), (1, 0)])
    chip, core_other = call(pair_kernel, place, (mine, other), (maps, maps))
    y1, y2, y3 = ring(chip, Y)
    group, before = call(
        group_kernel, place, (chip, y1, y2, y3), (maps, maps), [pltpu.VMEM((4, n + cols, n), F32)]
    )
    x1, x2, x3 = ring(group, X)
    forward = call(
        forward_kernel,
        place,
        (whole, core_other, before, x1, x2, x3, entry, rhs),
        of((here, cols, local), BF16),
    )
    gathered = exchange(jnp.broadcast_to(forward, (z, *forward.shape)), COL)
    c = cols // z
    applied, carried_parts = call(
        apply_kernel,
        place,
        (gathered, block_inverse, entry),
        (of((here, cols, local)), of((z, 2 * c, n))),
    )
    carried, send = call(
        back_kernel,
        place,
        (exchange(carried_parts, COL), whole, core_other, before),
        (of((2 * c, n)), of((chain, c, n))),
    )
    behind = call(
        behind_kernel,
        place,
        (exchange(send, CHAIN), carried, whole, core_other, y1, y2, y3, x1, x2, x3),
        of((z, 2 * c, n)),
    )
    return call(
        final_kernel,
        place,
        (exchange(behind, COL), applied, exit_, arriving),
        of((here, cols, local)),
    )


def solution(mesh):
    torus = Mesh(mesh.devices.reshape(4, 4, 2, mesh.shape["col"]), (X, Y, CORE, COL))
    return jax.shard_map(
        shards,
        mesh=torus,
        in_specs=(
            P(CHAIN, None, COL),
            P(CHAIN, COL, None),
            P(CHAIN, COL, None),
            P(CHAIN, COL, None),
            P(None, COL),
        ),
        out_specs=P(CHAIN, None, COL),
        check_vma=False,
    )
```

```python
import jax
import jax.numpy as jnp
from jax import lax
from jax.experimental import pallas as pl
from jax.experimental.pallas import tpu as pltpu
from jax.sharding import Mesh
from jax.sharding import PartitionSpec as P

X, Y, CORE, COL = "chain_0", "chain_1", "chain_2", "col"
CHAIN = (X, Y, CORE)
F32 = jnp.float32
BF16 = jnp.bfloat16

NN = (((1,), (0,)), ((), ()))
NT = (((1,), (1,)), ((), ()))
TN = (((0,), (0,)), ((), ()))


def dot16(a, b, dims):
    return lax.dot_general(a, b, dims, preferred_element_type=F32)


def dot32(a, b, dims):
    return lax.dot_general(a, b, dims, precision=lax.Precision.HIGHEST, preferred_element_type=F32)


def dot32_16(a, b, dims):
    high = a.astype(BF16)
    rest = a - high.astype(F32)
    middle = rest.astype(BF16)
    low = (rest - middle.astype(F32)).astype(BF16)
    rows = a.shape[0]
    out = dot16(jnp.concatenate([high, middle, low], axis=0), b, dims)
    return (out[2 * rows :] + out[rows : 2 * rows]) + out[:rows]


def vmem():
    return pl.BlockSpec(memory_space=pltpu.VMEM)


def smem():
    return pl.BlockSpec(memory_space=pltpu.SMEM)


def hbm():
    return pl.BlockSpec(memory_space=pltpu.HBM)


def call(kernel, place, arrays, outs, scratch=(), specs=None, cost=None, room=40):
    return pl.pallas_call(
        kernel,
        out_shape=outs,
        in_specs=[smem()] + (specs or [vmem()] * len(arrays)),
        out_specs=jax.tree.map(lambda _: vmem(), outs),
        scratch_shapes=list(scratch),
        cost_estimate=cost and pl.CostEstimate(flops=cost, bytes_accessed=cost // 100, transcendentals=0),
        compiler_params=pltpu.CompilerParams(vmem_limit_bytes=room * 1024 * 1024),
    )(place, *arrays)


def of(shape, dtype=F32):
    return jax.ShapeDtypeStruct(shape, dtype)


def put(out, start, rows, value):
    groups = out.shape[0]
    out[:, start : start + rows, :] = value.reshape(groups, rows, value.shape[1])


def load_kernel(place, entry, exit_, rhs, previous, entry_v, exit_v, rhs_v, turned, out, previous_v, sems):
    copies = [
        pltpu.make_async_copy(source, target, sems.at[i])
        for i, (source, target) in enumerate(
            ((entry, entry_v), (exit_, exit_v), (rhs, rhs_v), (previous, previous_v))
        )
    ]
    for copy in copies:
        copy.start()
    for copy in copies:
        copy.wait()
    groups = out.shape[0]
    n = entry_v.shape[2] // groups
    c = rhs_v.shape[1] // groups
    put(out, 0, n, -dot16(entry_v[0], exit_v[1], TN))
    put(out, n, c, dot16(rhs_v[0], exit_v[1], NN))
    put(out, n + c, c, dot16(previous_v[...], exit_v[0], NN))
    both = jnp.concatenate([rhs_v[0], rhs_v[1]], axis=0).astype(F32)
    turned[...] = both.T


def partial_kernel(place, entry, arriving, rhs, early, out):
    groups = out.shape[0]
    n = entry.shape[2] // groups
    c = rhs.shape[1] // groups
    out[:, 0:n, :] = early[:, 0:n, :]
    put(out, n, n, -dot16(entry[1], arriving[0], TN))
    out[:, 2 * n : 2 * n + c, :] = early[:, n : n + c, :]
    put(out, 2 * n + c, c, dot16(rhs[1], arriving[0], NN))
    out[:, 2 * n + 2 * c :, :] = early[:, n + c :, :]


def sum_kernel(place, parts, out):
    total = parts[0]
    for k in range(1, parts.shape[0]):
        total = total + parts[k]
    for k in range(parts.shape[0]):
        out[k] = total


def pieces(whole):
    groups, rows, width = whole.shape
    n = width // groups
    c = (rows - 2 * n) // 3

    def take(start, count):
        return whole[:, start : start + count, :].reshape(groups * count, width)

    return take(0, n), take(n, n), take(2 * n, c), take(2 * n + c, c), take(2 * n + 2 * c, c)


def is_first(place):
    return (place[0] == 0) & (place[1] == 0) & (place[2] == 0)


def after(earlier, later, n):
    out = dot32(earlier, later[:n], NN)
    return out[:n], out[n:] + later[n:]


def local_kernel(place, whole, out):
    couple0, couple1, source0, source1, opening = pieces(whole)
    n = couple0.shape[0]
    folded = dot32(opening, couple0, NN) + source0
    source0 = jnp.where(is_first(place), folded, source0)
    out[:n] = dot32(couple0, couple1, NN)
    out[n:] = dot32(source0, couple1, NN) + source1


def pair_kernel(place, mine, other, out):
    n = mine.shape[1]
    upper = place[2] == 1
    first = jnp.where(upper, other[...], mine[...])
    second = jnp.where(upper, mine[...], other[...])
    out[:n], out[n:] = after(first, second, n)


def group_kernel(place, mine, one, two, three, total, before, slots):
    n = mine.shape[1]
    y = place[1]
    for d, ref in enumerate((mine, one, two, three)):
        slots[lax.rem(y - d + 4, 4)] = ref[...]

    low_top, low_bottom = after(slots[0], slots[1], n)
    high_top, high_bottom = after(slots[2], slots[3], n)
    low = jnp.concatenate([low_top, low_bottom], axis=0)
    out = dot32(low, high_top, NN)
    total[:n] = out[:n]
    total[n:] = out[n:] + high_bottom
    rows = lax.broadcasted_iota(jnp.int32, mine.shape, 0)
    lanes = lax.broadcasted_iota(jnp.int32, mine.shape, 1)

    @pl.when(y == 0)
    def _():
        before[...] = jnp.where(rows == lanes, 1.0, 0.0).astype(F32)

    @pl.when(y == 1)
    def _():
        before[...] = slots[0]

    @pl.when(y == 2)
    def _():
        before[...] = low

    @pl.when(y == 3)
    def _():
        out = dot32(low, slots[2, :n], NN)
        before[:n] = out[:n]
        before[n:] = out[n:] + slots[2, n:]


def tail_kernel(place, whole, other, before, maps, shifts):
    couple0, _, source0, _, opening = pieces(whole)
    n = couple0.shape[0]
    reach, shift = after(before[...], other[...], n)
    upper = place[2] == 1
    reach = jnp.where(upper, reach, before[:n])
    shift = jnp.where(upper, shift, before[n:])
    shift = jnp.where(is_first(place), opening, shift)
    out = dot32(jnp.concatenate([reach, shift], axis=0), couple0, NN)
    maps[:, :n] = reach
    maps[:, n:] = out[:n]
    shifts[:, :n] = shift
    shifts[:, n:] = out[n:] + source0


def forward_kernel(place, maps, shifts, one, two, three, entry, turned, out):
    n = one.shape[1]
    x = place[0]
    state = jnp.where(3 <= x, three[n:], 0.0)
    state = jnp.where(2 <= x, dot32(state, two[:n], NN) + two[n:], state)
    state = jnp.where(1 <= x, dot32(state, one[:n], NN) + one[n:], state)
    both = dot32(state, maps[...], NN) + shifts[...]
    states = jnp.concatenate([both[:, :n], both[:, n:]], axis=0)
    high = states.astype(BF16)
    rest = states - high.astype(F32)
    middle = rest.astype(BF16)
    low = (rest - middle.astype(F32)).astype(BF16)
    lanes = lax.broadcasted_iota(jnp.int32, out.shape, 1)

    def through(i):
        return (dot16(entry[i], low, NT) + dot16(entry[i], middle, NT)) + dot16(entry[i], high, NT)

    product = jnp.where(lanes < both.shape[0], through(0), through(1))
    out[...] = (turned[...] - product).astype(BF16)


def apply_kernel(place, forward, inverse, entry, applied, carried):
    groups, local, both = forward.shape
    whole = forward[...].reshape(groups * local, both)
    lanes = lax.broadcasted_iota(jnp.int32, applied.shape, 1)
    half = both // 2
    value = jnp.where(lanes < half, dot16(inverse[0], whole, NN), dot16(inverse[1], whole, NN))
    applied[...] = value
    low = value.astype(BF16)
    c = half // groups
    put(carried, 0, c, dot16(low, entry[0], TN)[:half])
    put(carried, c, c, dot16(low, entry[1], TN)[half:])


def routes_kernel(place, whole, other, before, y1, y2, y3, x1, x2, x3, leave, reach):
    couple0, couple1, _, _, _ = pieces(whole)
    n = couple0.shape[0]
    rows = lax.broadcasted_iota(jnp.int32, (n, n), 0)
    lanes = lax.broadcasted_iota(jnp.int32, (n, n), 1)
    identity = jnp.where(rows == lanes, 1.0, 0.0).astype(F32)
    x, y, core = place[0], place[1], place[2]
    lower = jnp.where(core == 1, other[:n], identity)
    out = dot32(lower, couple0, NN)
    chip = jnp.concatenate([lower, out], axis=1)
    leave[0:n, :n] = identity
    leave[0:n, n:] = couple0
    leave[n : 2 * n, :] = chip
    leave[2 * n : 3 * n, :] = dot32(before[:n], chip, NN)
    here = jnp.where(core == 0, other[:n], identity)
    blocks = [identity]
    for e, ref in ((1, y3), (2, y2), (3, y1)):
        blocks.append(here)
        here = jnp.where(y + e <= 3, dot32(here, ref[:n], NN), here)
    for e, ref in ((1, x3), (2, x2), (3, x1)):
        blocks.append(here)
        if e < 3:
            here = dot32(here, ref[:n], NN)
    stacked = jnp.concatenate(blocks, axis=1)
    reach[:n, :] = stacked
    reach[n:, :] = dot32(couple1, stacked, NN)


def back_kernel(place, parts, leave, carried, send):
    c = parts.shape[1] // 2
    total = parts[0]
    for k in range(1, parts.shape[0]):
        total = total + parts[k]
    carried[...] = total
    n = total.shape[1]
    x, y = place[0], place[1]
    values = dot32(jnp.concatenate([total[:c], total[c:]], axis=1), leave[...], NT)
    own, chip, group = values[:, :n], values[:, n : 2 * n], values[:, 2 * n :]
    for k in range(send.shape[0]):
        same_x = x == k // 8
        same_y = y == (k // 2) % 4
        send[k] = jnp.where(same_x, jnp.where(same_y, own, chip), group)


def behind_kernel(place, got, carried, reach, out):
    n = carried.shape[1]
    c = carried.shape[0] // 2
    x, y, core = place[0], place[1], place[2]
    terms = [jnp.where(core == 0, got[x * 8 + y * 2 + 1], 0.0)]
    for e in (1, 2, 3):
        base = x * 8 + lax.rem(y + e, 4) * 2
        terms.append(jnp.where(y + e <= 3, got[base] + got[base + 1], 0.0))
    for e in (1, 2, 3):
        base = lax.rem(x + e, 4) * 8
        extra = got[base]
        for k in range(1, 8):
            extra = extra + got[base + k]
        terms.append(jnp.where(x + e <= 3, extra, 0.0))
    values = dot32(jnp.concatenate(terms, axis=1), reach[...], NT)
    state = values[:, :n]
    inner = values[:, n:] + carried[c:]
    for k in range(out.shape[0]):
        out[k, :c] = inner
        out[k, c:] = state


def final_kernel(place, got, applied, exit_, arriving, out):
    groups, rows, width = got.shape
    c = rows // 2
    inner = got[:, :c, :].reshape(groups * c, width)
    outer = got[:, c:, :].reshape(groups * c, width)
    turned = applied[...].T
    out[0] = turned[: groups * c] - dot32_16(inner, exit_[1], NT)
    out[1] = turned[groups * c :] - dot32_16(outer, arriving[0], NT)


def exchange(value, axes):
    return lax.all_to_all(value, axes, split_axis=0, concat_axis=0, tiled=True)


def ring(value, axis):
    size = lax.axis_size(axis)
    return [
        lax.ppermute(value, axis, [(i, (i + d) % size) for i in range(size)])
        for d in range(1, size)
    ]


def shards(rhs, block_inverse, entry, exit_, previous):
    z = lax.axis_size(COL)
    here, cols, local = rhs.shape
    n = entry.shape[2]
    place = jnp.stack([lax.axis_index(X), lax.axis_index(Y), lax.axis_index(CORE)]).astype(jnp.int32)
    chain = lax.axis_size(CHAIN)
    arriving = lax.ppermute(exit_[:1], CHAIN, [(i, i - 1) for i in range(1, chain)])
    rows = (2 * n + 3 * cols) // z
    entry_v, exit_v, rhs_v, turned, early = call(
        load_kernel,
        place,
        [pltpu.with_memory_space_constraint(a, pltpu.HBM) for a in (entry, exit_, rhs, previous)],
        (
            of(entry.shape, BF16),
            of(exit_.shape, BF16),
            of(rhs.shape, BF16),
            of((local, 2 * cols)),
            of((z, (n + 2 * cols) // z, n)),
        ),
        [pltpu.VMEM(previous.shape, BF16), pltpu.SemaphoreType.DMA((4,))],
        [hbm()] * 4,
        cost=1 << 28,
    )
    parts = call(partial_kernel, place, (entry_v, arriving, rhs_v, early), of((z, rows, n)))
    summed = call(sum_kernel, place, (exchange(parts, COL),), of((z, rows, n)))
    whole = exchange(summed, COL)
    maps = of((n + cols, n))
    mine = call(local_kernel, place, (whole,), maps)
    other = lax.ppermute(mine, CORE, [(0, 1), (1, 0)])
    chip = call(pair_kernel, place, (mine, other), maps)
    y1, y2, y3 = ring(chip, Y)
    group, before = call(
        group_kernel, place, (chip, y1, y2, y3), (maps, maps), [pltpu.VMEM((4, n + cols, n), F32)]
    )
    x1, x2, x3 = ring(group, X)
    ahead, shifts = call(
        tail_kernel, place, (whole, other, before), (of((n, 2 * n)), of((cols, 2 * n))), cost=1 << 27
    )
    forward = call(
        forward_kernel,
        place,
        (ahead, shifts, x1, x2, x3, entry_v, turned),
        of((local, 2 * cols), BF16),
    )
    leave, reach = call(
        routes_kernel,
        place,
        (whole, other, before, y1, y2, y3, x1, x2, x3),
        (of((3 * n, 2 * n)), of((2 * n, 7 * n))),
        cost=1 << 29,
    )
    gathered = exchange(jnp.broadcast_to(forward, (z, *forward.shape)), COL)
    c = cols // z
    applied, carried_parts = call(
        apply_kernel,
        place,
        (gathered, block_inverse, entry_v),
        (of((local, 2 * cols)), of((z, 2 * c, n))),
    )
    carried, send = call(
        back_kernel,
        place,
        (exchange(carried_parts, COL), leave),
        (of((2 * c, n)), of((chain, c, n))),
    )
    behind = call(
        behind_kernel, place, (exchange(send, CHAIN), carried, reach), of((z, 2 * c, n))
    )
    return call(
        final_kernel,
        place,
        (exchange(behind, COL), applied, exit_v, arriving),
        of((here, cols, local)),
    )


def solution(mesh):
    torus = Mesh(mesh.devices.reshape(4, 4, 2, mesh.shape["col"]), (X, Y, CORE, COL))
    return jax.shard_map(
        shards,
        mesh=torus,
        in_specs=(
            P(CHAIN, None, COL),
            P(CHAIN, COL, None),
            P(CHAIN, COL, None),
            P(CHAIN, COL, None),
            P(None, COL),
        ),
        out_specs=P(CHAIN, None, COL),
        check_vma=False,
    )
```

```python
import jax
import jax.numpy as jnp
from jax import lax
from jax.experimental import pallas as pl
from jax.experimental.pallas import tpu as pltpu
from jax.sharding import Mesh
from jax.sharding import PartitionSpec as P

X, Y, CORE, COL = "chain_0", "chain_1", "chain_2", "col"
CHAIN = (X, Y, CORE)
F32 = jnp.float32
BF16 = jnp.bfloat16

NN = (((1,), (0,)), ((), ()))
NT = (((1,), (1,)), ((), ()))
TN = (((0,), (0,)), ((), ()))


def dot16(a, b, dims):
    return lax.dot_general(a, b, dims, preferred_element_type=F32)


def dot32(a, b, dims):
    return lax.dot_general(a, b, dims, precision=lax.Precision.HIGHEST, preferred_element_type=F32)


def dot32_16(a, b, dims):
    high = a.astype(BF16)
    rest = a - high.astype(F32)
    middle = rest.astype(BF16)
    low = (rest - middle.astype(F32)).astype(BF16)
    rows = a.shape[0]
    out = dot16(jnp.concatenate([high, middle, low], axis=0), b, dims)
    return (out[2 * rows :] + out[rows : 2 * rows]) + out[:rows]


def three_parts(a):
    high = a.astype(BF16).astype(F32)
    middle = (a - high).astype(BF16).astype(F32)
    return high, middle, (a - high) - middle


def store_parts(ref, value):
    for k, part in enumerate(three_parts(value)):
        ref[k] = part.astype(BF16)


def dot_parts(a, b, dims):
    rows = a.shape[0]
    parts = jnp.concatenate(three_parts(a), axis=0)
    by_high = dot16(parts.astype(BF16), b[0], dims)
    by_middle = dot16(parts[: 2 * rows].astype(BF16), b[1], dims)
    by_low = dot16(parts[:rows].astype(BF16), b[2], dims)
    small = (by_low + by_middle[rows:]) + by_high[2 * rows :]
    return (small + (by_middle[:rows] + by_high[rows : 2 * rows])) + by_high[:rows]


def vmem():
    return pl.BlockSpec(memory_space=pltpu.VMEM)


def smem():
    return pl.BlockSpec(memory_space=pltpu.SMEM)


def hbm():
    return pl.BlockSpec(memory_space=pltpu.HBM)


def call(kernel, place, arrays, outs, scratch=(), specs=None, cost=None, room=24):
    return pl.pallas_call(
        kernel,
        out_shape=outs,
        in_specs=[smem()] + (specs or [vmem()] * len(arrays)),
        out_specs=jax.tree.map(lambda _: vmem(), outs),
        scratch_shapes=list(scratch),
        cost_estimate=cost and pl.CostEstimate(flops=cost, bytes_accessed=cost // 100, transcendentals=0),
        compiler_params=pltpu.CompilerParams(vmem_limit_bytes=room * 1024 * 1024),
    )(place, *arrays)


def of(shape, dtype=F32):
    return jax.ShapeDtypeStruct(shape, dtype)


def put(out, start, rows, value):
    groups = out.shape[0]
    out[:, start : start + rows, :] = value.reshape(groups, rows, value.shape[1])


def load_kernel(place, entry, exit_, rhs, previous, entry_v, exit_v, second, turned, out, rhs_v, previous_v, sems):
    copies = [
        pltpu.make_async_copy(source, target, sems.at[i])
        for i, (source, target) in enumerate(
            ((entry, entry_v), (exit_, exit_v), (rhs, rhs_v), (previous, previous_v))
        )
    ]
    for copy in copies:
        copy.start()
    for copy in copies:
        copy.wait()
    groups = out.shape[0]
    n = entry_v.shape[2] // groups
    c = rhs_v.shape[1] // groups
    put(out, 0, n, -dot16(entry_v[0], exit_v[1], TN))
    put(out, n, c, dot16(rhs_v[0], exit_v[1], NN))
    last = is_last(place)
    second[...] = jnp.where(last, previous_v[...].astype(F32), rhs_v[1].astype(F32)).astype(BF16)
    both = jnp.concatenate([rhs_v[0], rhs_v[1]], axis=0).astype(F32)
    turned[...] = both.T


def partial_kernel(place, entry, arriving, second, early, out):
    groups = out.shape[0]
    n = entry.shape[2] // groups
    c = second.shape[0] // groups
    out[:, 0:n, :] = early[:, 0:n, :]
    put(out, n, n, jnp.where(is_last(place), 0.0, -dot16(entry[1], arriving[0], TN)))
    out[:, 2 * n : 2 * n + c, :] = early[:, n : n + c, :]
    put(out, 2 * n + c, c, dot16(second[...], arriving[0], NN))


def sum_kernel(place, parts, out):
    total = parts[0]
    for k in range(1, parts.shape[0]):
        total = total + parts[k]
    for k in range(parts.shape[0]):
        out[k] = total


def pieces(whole):
    groups, rows, width = whole.shape
    n = width // groups
    c = (rows - 2 * n) // 2

    def take(start, count):
        return whole[:, start : start + count, :].reshape(groups * count, width)

    return take(0, n), take(n, n), take(2 * n, c), take(2 * n + c, c)


def is_last(place):
    return (place[0] == 3) & (place[1] == 3) & (place[2] == 1)


def after(earlier, later, n):
    out = dot32(earlier, later[:n], NN)
    return out[:n], out[n:] + later[n:]


def pair_kernel(place, mine, other, out, beside):
    def own(whole):
        couple0, couple1, source0, source1 = pieces(whole)
        top, bottom = after(
            jnp.concatenate([couple0, source0], axis=0),
            jnp.concatenate([couple1, source1], axis=0),
            couple0.shape[0],
        )
        return jnp.concatenate([top, bottom], axis=0)

    here, there = own(mine), own(other)
    n = here.shape[1]
    upper = place[2] == 1
    first = jnp.where(upper, there, here)
    second = jnp.where(upper, here, there)
    out[:n], out[n:] = after(first, second, n)
    beside[...] = there


def group_kernel(place, mine, one, two, three, total, before, slots):
    n = mine.shape[1]
    y = place[1]
    for d, ref in enumerate((mine, one, two, three)):
        slots[lax.rem(y - d + 4, 4)] = ref[...]

    low_top, low_bottom = after(slots[0], slots[1], n)
    high_top, high_bottom = after(slots[2], slots[3], n)
    low = jnp.concatenate([low_top, low_bottom], axis=0)
    out = dot32(low, high_top, NN)
    total[:n] = out[:n]
    total[n:] = out[n:] + high_bottom
    rows = lax.broadcasted_iota(jnp.int32, mine.shape, 0)
    lanes = lax.broadcasted_iota(jnp.int32, mine.shape, 1)

    @pl.when(y == 0)
    def _():
        before[...] = jnp.where(rows == lanes, 1.0, 0.0).astype(F32)

    @pl.when(y == 1)
    def _():
        before[...] = slots[0]

    @pl.when(y == 2)
    def _():
        before[...] = low

    @pl.when(y == 3)
    def _():
        out = dot32(low, slots[2, :n], NN)
        before[:n] = out[:n]
        before[n:] = out[n:] + slots[2, n:]


def tail_kernel(place, whole, other, before, maps, shifts):
    couple0, _, source0, _ = pieces(whole)
    n = couple0.shape[0]
    reach, shift = after(before[...], other[...], n)
    upper = place[2] == 1
    reach = jnp.where(upper, reach, before[:n])
    shift = jnp.where(upper, shift, before[n:])
    out = dot32(jnp.concatenate([reach, shift], axis=0), couple0, NN)
    maps[:, :n] = reach
    maps[:, n:] = out[:n]
    shifts[:, :n] = shift
    shifts[:, n:] = out[n:] + source0


def forward_kernel(place, maps, shifts, own, one, two, three, entry, turned, out):
    n = one.shape[1]
    x = place[0]
    state = jnp.where(x == 3, own[n:], 0.0)
    for d, ref in ((3, three), (2, two), (1, one)):
        state = jnp.where(d <= x + 1, dot32(state, ref[:n], NN) + ref[n:], state)
    both = dot32(state, maps[...], NN) + shifts[...]
    states = jnp.concatenate([both[:, :n], both[:, n:]], axis=0)
    high, middle, low = (part.astype(BF16) for part in three_parts(states))
    factor = jnp.concatenate(
        [
            jnp.concatenate([high, low], axis=1),
            jnp.concatenate([middle, jnp.zeros_like(middle)], axis=1),
        ],
        axis=0,
    )
    lanes = lax.broadcasted_iota(jnp.int32, out.shape, 1)
    width = states.shape[0]

    def through(i):
        product = dot16(jnp.concatenate([entry[i], entry[i]], axis=1), factor, NT)
        return product[:, width:] + product[:, :width]

    product = jnp.where(lanes < width // 2, through(0), through(1))
    out[...] = (turned[...] - product).astype(BF16)


def apply_kernel(place, forward, inverse, entry, applied, carried):
    groups, local, both = forward.shape
    whole = forward[...].reshape(groups * local, both)
    lanes = lax.broadcasted_iota(jnp.int32, applied.shape, 1)
    half = both // 2
    value = jnp.where(lanes < half, dot16(inverse[0], whole, NN), dot16(inverse[1], whole, NN))
    applied[...] = value
    low = value.astype(BF16)
    c = half // groups
    put(carried, 0, c, dot16(low, entry[0], TN)[:half])
    put(carried, c, c, dot16(low, entry[1], TN)[half:])


def routes_kernel(place, whole, other, before, y1, y2, y3, x1, x2, x3, applied, leave, reach, turned):
    couple0, couple1, _, _ = pieces(whole)
    turned[...] = applied[...].T
    n = couple0.shape[0]
    rows = lax.broadcasted_iota(jnp.int32, (n, n), 0)
    lanes = lax.broadcasted_iota(jnp.int32, (n, n), 1)
    identity = jnp.where(rows == lanes, 1.0, 0.0).astype(F32)
    x, y, core = place[0], place[1], place[2]
    lower = jnp.where(core == 1, other[:n], identity)
    out = dot32(lower, couple0, NN)
    chip = jnp.concatenate([lower, out], axis=1)
    top = jnp.concatenate([identity, couple0], axis=1)
    store_parts(leave, jnp.concatenate([top, chip, dot32(before[:n], chip, NN)], axis=0))
    here = jnp.where(core == 0, other[:n], identity)
    blocks = [identity]
    for e, ref in ((1, y3), (2, y2), (3, y1)):
        blocks.append(here)
        here = jnp.where(y + e <= 3, dot32(here, ref[:n], NN), here)
    for e, ref in ((1, x3), (2, x2), (3, x1)):
        blocks.append(here)
        if e < 3:
            here = dot32(here, ref[:n], NN)
    stacked = jnp.concatenate(blocks, axis=1)
    store_parts(reach, jnp.concatenate([stacked, dot32(couple1, stacked, NN)], axis=0))


def back_kernel(place, parts, leave, carried, send):
    c = parts.shape[1] // 2
    total = parts[0]
    for k in range(1, parts.shape[0]):
        total = total + parts[k]
    carried[...] = total
    n = total.shape[1]
    x, y = place[0], place[1]
    values = dot_parts(jnp.concatenate([total[:c], total[c:]], axis=1), leave, NT)
    own, chip, group = values[:, :n], values[:, n : 2 * n], values[:, 2 * n :]
    for k in range(send.shape[0]):
        same_x = x == k // 8
        same_y = y == (k // 2) % 4
        send[k] = jnp.where(same_x, jnp.where(same_y, own, chip), group)


def behind_kernel(place, got, carried, reach, out):
    n = carried.shape[1]
    c = carried.shape[0] // 2
    x, y, core = place[0], place[1], place[2]
    terms = [jnp.where(core == 0, got[x * 8 + y * 2 + 1], 0.0)]
    for e in (1, 2, 3):
        base = x * 8 + lax.rem(y + e, 4) * 2
        terms.append(jnp.where(y + e <= 3, got[base] + got[base + 1], 0.0))
    for e in (1, 2, 3):
        base = lax.rem(x + e, 4) * 8
        extra = got[base]
        for k in range(1, 8):
            extra = extra + got[base + k]
        terms.append(jnp.where(x + e <= 3, extra, 0.0))
    values = dot_parts(jnp.concatenate(terms, axis=1), reach, NT)
    state = values[:, :n]
    inner = values[:, n:] + carried[c:]
    for k in range(out.shape[0]):
        out[k, :c] = inner
        out[k, c:] = state


def final_kernel(place, got, turned, exit_, arriving, out):
    groups, rows, width = got.shape
    c = rows // 2
    inner = got[:, :c, :].reshape(groups * c, width)
    outer = got[:, c:, :].reshape(groups * c, width)
    out[0] = turned[: groups * c] - dot32_16(inner, exit_[1], NT)
    out[1] = turned[groups * c :] - dot32_16(outer, arriving[0], NT)


def exchange(value, axes):
    return lax.all_to_all(value, axes, split_axis=0, concat_axis=0, tiled=True)


def ring(value, axis):
    size = lax.axis_size(axis)
    return [
        lax.ppermute(value, axis, [(i, (i + d) % size) for i in range(size)])
        for d in range(1, size)
    ]


def shards(rhs, block_inverse, entry, exit_, previous):
    z = lax.axis_size(COL)
    here, cols, local = rhs.shape
    n = entry.shape[2]
    place = jnp.stack([lax.axis_index(X), lax.axis_index(Y), lax.axis_index(CORE)]).astype(jnp.int32)
    chain = lax.axis_size(CHAIN)
    arriving = lax.ppermute(exit_[:1], CHAIN, [(i, (i - 1) % chain) for i in range(chain)])
    rows = (2 * n + 2 * cols) // z
    entry_v, exit_v, second, turned, early = call(
        load_kernel,
        place,
        [pltpu.with_memory_space_constraint(a, pltpu.HBM) for a in (entry, exit_, rhs, previous)],
        (
            of(entry.shape, BF16),
            of(exit_.shape, BF16),
            of(previous.shape, BF16),
            of((local, 2 * cols)),
            of((z, (n + cols) // z, n)),
        ),
        [
            pltpu.VMEM(rhs.shape, BF16),
            pltpu.VMEM(previous.shape, BF16),
            pltpu.SemaphoreType.DMA((4,)),
        ],
        [hbm()] * 4,
        cost=1 << 28,
    )
    parts = call(partial_kernel, place, (entry_v, arriving, second, early), of((z, rows, n)))
    summed = call(sum_kernel, place, (exchange(parts, COL),), of((z, rows, n)))
    whole = exchange(summed, COL)
    maps = of((n + cols, n))
    whole_other = lax.ppermute(whole, CORE, [(0, 1), (1, 0)])
    chip, other = call(pair_kernel, place, (whole, whole_other), (maps, maps))
    y1, y2, y3 = ring(chip, Y)
    group, before = call(
        group_kernel, place, (chip, y1, y2, y3), (maps, maps), [pltpu.VMEM((4, n + cols, n), F32)]
    )
    x1, x2, x3 = ring(group, X)
    ahead, shifts = call(
        tail_kernel, place, (whole, other, before), (of((n, 2 * n)), of((cols, 2 * n))), cost=1 << 27
    )
    forward = call(
        forward_kernel,
        place,
        (ahead, shifts, group, x1, x2, x3, entry_v, turned),
        of((local, 2 * cols), BF16),
    )
    gathered = exchange(jnp.broadcast_to(forward, (z, *forward.shape)), COL)
    c = cols // z
    applied, carried_parts = call(
        apply_kernel,
        place,
        (gathered, block_inverse, entry_v),
        (of((local, 2 * cols)), of((z, 2 * c, n))),
    )
    leave, reach, applied_turned = call(
        routes_kernel,
        place,
        (whole, other, before, y1, y2, y3, x1, x2, x3, applied),
        (of((3, 3 * n, 2 * n), BF16), of((3, 2 * n, 7 * n), BF16), of((2 * cols, local))),
        cost=1 << 29,
    )
    carried, send = call(
        back_kernel,
        place,
        (exchange(carried_parts, COL), leave),
        (of((2 * c, n)), of((chain, c, n))),
    )
    behind = call(
        behind_kernel, place, (exchange(send, CHAIN), carried, reach), of((z, 2 * c, n))
    )
    return call(
        final_kernel,
        place,
        (exchange(behind, COL), applied_turned, exit_v, arriving),
        of((here, cols, local)),
    )


def solution(mesh):
    torus = Mesh(mesh.devices.reshape(4, 4, 2, mesh.shape["col"]), (X, Y, CORE, COL))
    return jax.shard_map(
        shards,
        mesh=torus,
        in_specs=(
            P(CHAIN, None, COL),
            P(CHAIN, COL, None),
            P(CHAIN, COL, None),
            P(CHAIN, COL, None),
            P(None, COL),
        ),
        out_specs=P(CHAIN, None, COL),
        check_vma=False,
    )
```

```python
import jax
import jax.numpy as jnp
from jax import lax
from jax.experimental import pallas as pl
from jax.experimental.pallas import tpu as pltpu
from jax.sharding import Mesh
from jax.sharding import PartitionSpec as P

X, Y, CORE, COL = "chain_0", "chain_1", "chain_2", "col"
CHAIN = (X, Y, CORE)
F32 = jnp.float32
BF16 = jnp.bfloat16

NN = (((1,), (0,)), ((), ()))
NT = (((1,), (1,)), ((), ()))
TN = (((0,), (0,)), ((), ()))


def dot16(a, b, dims):
    return lax.dot_general(a, b, dims, preferred_element_type=F32)


def dot32(a, b, dims):
    return lax.dot_general(a, b, dims, precision=lax.Precision.HIGHEST, preferred_element_type=F32)


def dot32_16(a, b, dims):
    high = a.astype(BF16)
    rest = a - high.astype(F32)
    middle = rest.astype(BF16)
    low = (rest - middle.astype(F32)).astype(BF16)
    rows = a.shape[0]
    out = dot16(jnp.concatenate([high, middle, low], axis=0), b, dims)
    return (out[2 * rows :] + out[rows : 2 * rows]) + out[:rows]


def three_parts(a):
    high = a.astype(BF16).astype(F32)
    middle = (a - high).astype(BF16).astype(F32)
    return high, middle, (a - high) - middle


def store_parts(ref, value):
    for k, part in enumerate(three_parts(value)):
        ref[k] = part.astype(BF16)


def dot_parts(a, b, dims):
    rows = a.shape[0]
    parts = jnp.concatenate(three_parts(a), axis=0)
    by_high = dot16(parts.astype(BF16), b[0], dims)
    by_middle = dot16(parts[: 2 * rows].astype(BF16), b[1], dims)
    by_low = dot16(parts[:rows].astype(BF16), b[2], dims)
    small = (by_low + by_middle[rows:]) + by_high[2 * rows :]
    return (small + (by_middle[:rows] + by_high[rows : 2 * rows])) + by_high[:rows]


def vmem():
    return pl.BlockSpec(memory_space=pltpu.VMEM)


def smem():
    return pl.BlockSpec(memory_space=pltpu.SMEM)


def hbm():
    return pl.BlockSpec(memory_space=pltpu.HBM)


def call(kernel, place, arrays, outs, scratch=(), specs=None, cost=None, room=24):
    return pl.pallas_call(
        kernel,
        out_shape=outs,
        in_specs=[smem()] + (specs or [vmem()] * len(arrays)),
        out_specs=jax.tree.map(lambda _: vmem(), outs),
        scratch_shapes=list(scratch),
        cost_estimate=cost and pl.CostEstimate(flops=cost, bytes_accessed=cost // 100, transcendentals=0),
        compiler_params=pltpu.CompilerParams(vmem_limit_bytes=room * 1024 * 1024),
    )(place, *arrays)


def of(shape, dtype=F32):
    return jax.ShapeDtypeStruct(shape, dtype)


def put(out, start, rows, value):
    groups = out.shape[0]
    out[:, start : start + rows, :] = value.reshape(groups, rows, value.shape[1])


def load_kernel(place, entry, exit_, rhs, previous, entry_v, exit_v, second, turned, out, rhs_v, previous_v, sems):
    copies = [
        pltpu.make_async_copy(source, target, sems.at[i])
        for i, (source, target) in enumerate(
            ((entry, entry_v), (exit_, exit_v), (rhs, rhs_v), (previous, previous_v))
        )
    ]
    for copy in copies:
        copy.start()
    for copy in copies:
        copy.wait()
    groups = out.shape[0]
    n = entry_v.shape[2] // groups
    c = rhs_v.shape[1] // groups
    put(out, 0, n, -dot16(entry_v[0], exit_v[1], TN))
    put(out, n, c, dot16(rhs_v[0], exit_v[1], NN))
    last = is_last(place)
    second[...] = jnp.where(last, previous_v[...].astype(F32), rhs_v[1].astype(F32)).astype(BF16)
    both = jnp.concatenate([rhs_v[0], rhs_v[1]], axis=0).astype(F32)
    turned[...] = both.T


def partial_kernel(place, entry, arriving, second, early, out):
    groups = out.shape[0]
    n = entry.shape[2] // groups
    c = second.shape[0] // groups
    out[:, 0:n, :] = early[:, 0:n, :]
    put(out, n, n, jnp.where(is_last(place), 0.0, -dot16(entry[1], arriving[0], TN)))
    out[:, 2 * n : 2 * n + c, :] = early[:, n : n + c, :]
    put(out, 2 * n + c, c, dot16(second[...], arriving[0], NN))


def sum_kernel(place, parts, out):
    total = parts[0]
    for k in range(1, parts.shape[0]):
        total = total + parts[k]
    for k in range(parts.shape[0]):
        out[k] = total


def pieces(whole):
    groups, rows, width = whole.shape
    n = width // groups
    c = (rows - 2 * n) // 2

    def take(start, count):
        return whole[:, start : start + count, :].reshape(groups * count, width)

    return take(0, n), take(n, n), take(2 * n, c), take(2 * n + c, c)


def is_last(place):
    return (place[0] == 3) & (place[1] == 3) & (place[2] == 1)


def after(earlier, later, n):
    out = dot32(earlier, later[:n], NN)
    return out[:n], out[n:] + later[n:]


def pair_kernel(place, mine, other, out, beside):
    def own(whole):
        couple0, couple1, source0, source1 = pieces(whole)
        top, bottom = after(
            jnp.concatenate([couple0, source0], axis=0),
            jnp.concatenate([couple1, source1], axis=0),
            couple0.shape[0],
        )
        return jnp.concatenate([top, bottom], axis=0)

    here, there = own(mine), own(other)
    n = here.shape[1]
    upper = place[2] == 1
    first = jnp.where(upper, there, here)
    second = jnp.where(upper, here, there)
    out[:n], out[n:] = after(first, second, n)
    beside[...] = there


def group_kernel(place, mine, one, two, three, total, before, slots):
    n = mine.shape[1]
    y = place[1]
    for d, ref in enumerate((mine, one, two, three)):
        slots[lax.rem(y - d + 4, 4)] = ref[...]

    low_top, low_bottom = after(slots[0], slots[1], n)
    high_top, high_bottom = after(slots[2], slots[3], n)
    low = jnp.concatenate([low_top, low_bottom], axis=0)
    out = dot32(low, high_top, NN)
    total[:n] = out[:n]
    total[n:] = out[n:] + high_bottom
    rows = lax.broadcasted_iota(jnp.int32, mine.shape, 0)
    lanes = lax.broadcasted_iota(jnp.int32, mine.shape, 1)

    @pl.when(y == 0)
    def _():
        before[...] = jnp.where(rows == lanes, 1.0, 0.0).astype(F32)

    @pl.when(y == 1)
    def _():
        before[...] = slots[0]

    @pl.when(y == 2)
    def _():
        before[...] = low

    @pl.when(y == 3)
    def _():
        out = dot32(low, slots[2, :n], NN)
        before[:n] = out[:n]
        before[n:] = out[n:] + slots[2, n:]


def tail_kernel(place, whole, other, before, maps, shifts):
    couple0, _, source0, _ = pieces(whole)
    n = couple0.shape[0]
    reach, shift = after(before[...], other[...], n)
    upper = place[2] == 1
    reach = jnp.where(upper, reach, before[:n])
    shift = jnp.where(upper, shift, before[n:])
    out = dot32(jnp.concatenate([reach, shift], axis=0), couple0, NN)
    maps[:, :n] = reach
    maps[:, n:] = out[:n]
    shifts[:, :n] = shift
    shifts[:, n:] = out[n:] + source0


def forward_kernel(place, maps, shifts, own, one, two, three, entry, turned, out):
    n = one.shape[1]
    x = place[0]
    state = jnp.where(x == 3, own[n:], 0.0)
    for d, ref in ((3, three), (2, two), (1, one)):
        state = jnp.where(d <= x + 1, dot32(state, ref[:n], NN) + ref[n:], state)
    both = dot32(state, maps[...], NN) + shifts[...]
    states = jnp.concatenate([both[:, :n], both[:, n:]], axis=0)
    high, middle, low = (part.astype(BF16) for part in three_parts(states))
    factor = jnp.concatenate(
        [
            jnp.concatenate([high, low], axis=1),
            jnp.concatenate([middle, jnp.zeros_like(middle)], axis=1),
        ],
        axis=0,
    )
    lanes = lax.broadcasted_iota(jnp.int32, out.shape, 1)
    width = states.shape[0]

    def through(i):
        product = dot16(jnp.concatenate([entry[i], entry[i]], axis=1), factor, NT)
        return product[:, width:] + product[:, :width]

    product = jnp.where(lanes < width // 2, through(0), through(1))
    out[...] = (turned[...] - product).astype(BF16)


def apply_kernel(place, *refs):
    groups = len(refs) - 5
    blocks = refs[:groups]
    inverse, entry, turned, carried, slots = refs[groups:]
    local, both = blocks[0].shape
    for d, block in enumerate(blocks):
        slots[lax.rem(place[3] - d + groups, groups)] = block[...]
    whole = slots[...].reshape(groups * local, both)
    lanes = lax.broadcasted_iota(jnp.int32, (local, both), 1)
    half = both // 2
    value = jnp.where(lanes < half, dot16(inverse[0], whole, NN), dot16(inverse[1], whole, NN))
    turned[...] = value.T
    low = value.astype(BF16)
    c = half // groups
    put(carried, 0, c, dot16(low, entry[0], TN)[:half])
    put(carried, c, c, dot16(low, entry[1], TN)[half:])


def routes_kernel(place, whole, other, before, y1, y2, y3, x1, x2, x3, leave, reach):
    couple0, couple1, _, _ = pieces(whole)
    n = couple0.shape[0]
    rows = lax.broadcasted_iota(jnp.int32, (n, n), 0)
    lanes = lax.broadcasted_iota(jnp.int32, (n, n), 1)
    identity = jnp.where(rows == lanes, 1.0, 0.0).astype(F32)
    x, y, core = place[0], place[1], place[2]
    lower = jnp.where(core == 1, other[:n], identity)
    out = dot32(lower, couple0, NN)
    chip = jnp.concatenate([lower, out], axis=1)
    top = jnp.concatenate([identity, couple0], axis=1)
    store_parts(leave, jnp.concatenate([top, chip, dot32(before[:n], chip, NN)], axis=0))
    here = jnp.where(core == 0, other[:n], identity)
    blocks = [identity]
    for e, ref in ((1, y3), (2, y2), (3, y1)):
        blocks.append(here)
        here = jnp.where(y + e <= 3, dot32(here, ref[:n], NN), here)
    for e, ref in ((1, x3), (2, x2), (3, x1)):
        blocks.append(here)
        if e < 3:
            here = dot32(here, ref[:n], NN)
    stacked = jnp.concatenate(blocks, axis=1)
    store_parts(reach, jnp.concatenate([stacked, dot32(couple1, stacked, NN)], axis=0))


def back_kernel(place, parts, leave, carried, send):
    c = parts.shape[1] // 2
    total = parts[0]
    for k in range(1, parts.shape[0]):
        total = total + parts[k]
    carried[...] = total
    n = total.shape[1]
    x, y = place[0], place[1]
    values = dot_parts(jnp.concatenate([total[:c], total[c:]], axis=1), leave, NT)
    own, chip, group = values[:, :n], values[:, n : 2 * n], values[:, 2 * n :]
    for k in range(send.shape[0]):
        same_x = x == k // 8
        same_y = y == (k // 2) % 4
        send[k] = jnp.where(same_x, jnp.where(same_y, own, chip), group)


def behind_kernel(place, got, carried, reach, out):
    n = carried.shape[1]
    c = carried.shape[0] // 2
    x, y, core = place[0], place[1], place[2]
    terms = [jnp.where(core == 0, got[x * 8 + y * 2 + 1], 0.0)]
    for e in (1, 2, 3):
        base = x * 8 + lax.rem(y + e, 4) * 2
        terms.append(jnp.where(y + e <= 3, got[base] + got[base + 1], 0.0))
    for e in (1, 2, 3):
        base = lax.rem(x + e, 4) * 8
        extra = got[base]
        for k in range(1, 8):
            extra = extra + got[base + k]
        terms.append(jnp.where(x + e <= 3, extra, 0.0))
    values = dot_parts(jnp.concatenate(terms, axis=1), reach, NT)
    state = values[:, :n]
    inner = values[:, n:] + carried[c:]
    for k in range(out.shape[0]):
        out[k, :c] = inner
        out[k, c:] = state


def final_kernel(place, got, turned, exit_, arriving, out):
    groups, rows, width = got.shape
    c = rows // 2
    inner = got[:, :c, :].reshape(groups * c, width)
    outer = got[:, c:, :].reshape(groups * c, width)
    out[0] = turned[: groups * c] - dot32_16(inner, exit_[1], NT)
    out[1] = turned[groups * c :] - dot32_16(outer, arriving[0], NT)


def exchange(value, axes):
    return lax.all_to_all(value, axes, split_axis=0, concat_axis=0, tiled=True)


def ring(value, axis):
    size = lax.axis_size(axis)
    return [
        lax.ppermute(value, axis, [(i, (i + d) % size) for i in range(size)])
        for d in range(1, size)
    ]


def shards(rhs, block_inverse, entry, exit_, previous):
    z = lax.axis_size(COL)
    here, cols, local = rhs.shape
    n = entry.shape[2]
    place = jnp.stack([lax.axis_index(X), lax.axis_index(Y), lax.axis_index(CORE), lax.axis_index(COL)]).astype(jnp.int32)
    chain = lax.axis_size(CHAIN)
    arriving = lax.ppermute(exit_[:1], CHAIN, [(i, (i - 1) % chain) for i in range(chain)])
    rows = (2 * n + 2 * cols) // z
    entry_v, exit_v, second, turned, early = call(
        load_kernel,
        place,
        [pltpu.with_memory_space_constraint(a, pltpu.HBM) for a in (entry, exit_, rhs, previous)],
        (
            of(entry.shape, BF16),
            of(exit_.shape, BF16),
            of(previous.shape, BF16),
            of((local, 2 * cols)),
            of((z, (n + cols) // z, n)),
        ),
        [
            pltpu.VMEM(rhs.shape, BF16),
            pltpu.VMEM(previous.shape, BF16),
            pltpu.SemaphoreType.DMA((4,)),
        ],
        [hbm()] * 4,
        cost=1 << 28,
    )
    parts = call(partial_kernel, place, (entry_v, arriving, second, early), of((z, rows, n)))
    summed = call(sum_kernel, place, (exchange(parts, COL),), of((z, rows, n)))
    whole = exchange(summed, COL)
    maps = of((n + cols, n))
    whole_other = lax.ppermute(whole, CORE, [(0, 1), (1, 0)])
    chip, other = call(pair_kernel, place, (whole, whole_other), (maps, maps))
    y1, y2, y3 = ring(chip, Y)
    group, before = call(
        group_kernel, place, (chip, y1, y2, y3), (maps, maps), [pltpu.VMEM((4, n + cols, n), F32)]
    )
    x1, x2, x3 = ring(group, X)
    ahead, shifts = call(
        tail_kernel, place, (whole, other, before), (of((n, 2 * n)), of((cols, 2 * n))), cost=1 << 27
    )
    forward = call(
        forward_kernel,
        place,
        (ahead, shifts, group, x1, x2, x3, entry_v, turned),
        of((local, 2 * cols), BF16),
    )
    up = [(i, (i + 1) % z) for i in range(z)]
    down = [(i, (i - 1) % z) for i in range(z)]
    far = [(i, (i + z // 2) % z) for i in range(z)]
    blocks = [forward] + [None] * (z - 1)
    blocks[1] = lax.ppermute(forward, COL, up)
    blocks[7] = lax.ppermute(forward, COL, down)
    blocks[4] = lax.ppermute(forward, COL, far)
    blocks[2] = lax.ppermute(blocks[1], COL, up)
    blocks[6] = lax.ppermute(blocks[7], COL, down)
    leave, reach = call(
        routes_kernel,
        place,
        (whole, other, before, y1, y2, y3, x1, x2, x3),
        (of((3, 3 * n, 2 * n), BF16), of((3, 2 * n, 7 * n), BF16)),
        cost=1 << 29,
    )
    blocks[2], blocks[6], leave, reach = lax.optimization_barrier((blocks[2], blocks[6], leave, reach))
    blocks[3] = lax.ppermute(blocks[2], COL, up)
    blocks[5] = lax.ppermute(blocks[6], COL, down)
    c = cols // z
    turned_applied, carried_parts = call(
        apply_kernel,
        place,
        (*blocks, block_inverse, entry_v),
        (of((2 * cols, local)), of((z, 2 * c, n))),
        [pltpu.VMEM((z, local, 2 * cols), BF16)],
    )
    carried, send = call(
        back_kernel,
        place,
        (exchange(carried_parts, COL), leave),
        (of((2 * c, n)), of((chain, c, n))),
    )
    behind = call(
        behind_kernel, place, (exchange(send, CHAIN), carried, reach), of((z, 2 * c, n))
    )
    return call(
        final_kernel,
        place,
        (exchange(behind, COL), turned_applied, exit_v, arriving),
        of((here, cols, local)),
    )


def solution(mesh):
    torus = Mesh(mesh.devices.reshape(4, 4, 2, mesh.shape["col"]), (X, Y, CORE, COL))
    return jax.shard_map(
        shards,
        mesh=torus,
        in_specs=(
            P(CHAIN, None, COL),
            P(CHAIN, COL, None),
            P(CHAIN, COL, None),
            P(CHAIN, COL, None),
            P(None, COL),
        ),
        out_specs=P(CHAIN, None, COL),
        check_vma=False,
    )
```

```python
import jax
import jax.numpy as jnp
from jax import lax
from jax.experimental import pallas as pl
from jax.experimental.pallas import tpu as pltpu
from jax.sharding import Mesh
from jax.sharding import PartitionSpec as P

X, Y, CORE, COL = "chain_0", "chain_1", "chain_2", "col"
CHAIN = (X, Y, CORE)
F32 = jnp.float32
BF16 = jnp.bfloat16

NN = (((1,), (0,)), ((), ()))
NT = (((1,), (1,)), ((), ()))
TN = (((0,), (0,)), ((), ()))


def dot16(a, b, dims):
    return lax.dot_general(a, b, dims, preferred_element_type=F32)


def dot32(a, b, dims):
    return dot_parts(a, [part.astype(BF16) for part in three_parts(b)], dims)


def dot32_16(a, b, dims):
    high = a.astype(BF16)
    rest = a - high.astype(F32)
    middle = rest.astype(BF16)
    low = (rest - middle.astype(F32)).astype(BF16)
    rows = a.shape[0]
    out = dot16(jnp.concatenate([high, middle, low], axis=0), b, dims)
    return (out[2 * rows :] + out[rows : 2 * rows]) + out[:rows]


def three_parts(a):
    high = a.astype(BF16).astype(F32)
    middle = (a - high).astype(BF16).astype(F32)
    return high, middle, (a - high) - middle


def store_parts(ref, value):
    for k, part in enumerate(three_parts(value)):
        ref[k] = part.astype(BF16)


def dot_parts(a, b, dims):
    rows = a.shape[0]
    parts = jnp.concatenate(three_parts(a), axis=0)
    by_high = dot16(parts.astype(BF16), b[0], dims)
    by_middle = dot16(parts[: 2 * rows].astype(BF16), b[1], dims)
    by_low = dot16(parts[:rows].astype(BF16), b[2], dims)
    small = (by_low + by_middle[rows:]) + by_high[2 * rows :]
    return (small + (by_middle[:rows] + by_high[rows : 2 * rows])) + by_high[:rows]


def vmem():
    return pl.BlockSpec(memory_space=pltpu.VMEM)


def smem():
    return pl.BlockSpec(memory_space=pltpu.SMEM)


def hbm():
    return pl.BlockSpec(memory_space=pltpu.HBM)


def call(kernel, place, arrays, outs, scratch=(), specs=None, cost=None, room=24):
    return pl.pallas_call(
        kernel,
        out_shape=outs,
        in_specs=[smem()] + (specs or [vmem()] * len(arrays)),
        out_specs=jax.tree.map(lambda _: vmem(), outs),
        scratch_shapes=list(scratch),
        cost_estimate=cost and pl.CostEstimate(flops=cost, bytes_accessed=cost // 100, transcendentals=0),
        compiler_params=pltpu.CompilerParams(vmem_limit_bytes=room * 1024 * 1024),
    )(place, *arrays)


def of(shape, dtype=F32):
    return jax.ShapeDtypeStruct(shape, dtype)


def put(out, start, rows, value):
    groups = out.shape[0]
    out[:, start : start + rows, :] = value.reshape(groups, rows, value.shape[1])


def load_kernel(place, entry, exit_, rhs, previous, entry_v, exit_v, second, turned, out, rhs_v, previous_v, sems):
    copies = [
        pltpu.make_async_copy(source, target, sems.at[i])
        for i, (source, target) in enumerate(
            ((entry, entry_v), (exit_, exit_v), (rhs, rhs_v), (previous, previous_v))
        )
    ]
    for copy in copies:
        copy.start()
    for copy in copies:
        copy.wait()
    groups = out.shape[0]
    n = entry_v.shape[2] // groups
    c = rhs_v.shape[1] // groups
    put(out, 0, n, -dot16(entry_v[0], exit_v[1], TN))
    put(out, n, c, dot16(rhs_v[0], exit_v[1], NN))
    last = is_last(place)
    second[...] = jnp.where(last, previous_v[...].astype(F32), rhs_v[1].astype(F32)).astype(BF16)
    both = jnp.concatenate([rhs_v[0], rhs_v[1]], axis=0).astype(F32)
    turned[...] = both.T


def partial_kernel(place, entry, arriving, second, early, out):
    groups = out.shape[0]
    n = entry.shape[2] // groups
    c = second.shape[0] // groups
    out[:, 0:n, :] = early[:, 0:n, :]
    put(out, n, n, jnp.where(is_last(place), 0.0, -dot16(entry[1], arriving[0], TN)))
    out[:, 2 * n : 2 * n + c, :] = early[:, n : n + c, :]
    put(out, 2 * n + c, c, dot16(second[...], arriving[0], NN))


def sum_kernel(place, parts, out):
    total = parts[0]
    for k in range(1, parts.shape[0]):
        total = total + parts[k]
    for k in range(parts.shape[0]):
        out[k] = total


def pieces(whole):
    groups, rows, width = whole.shape
    n = width // groups
    c = (rows - 2 * n) // 2

    def take(start, count):
        return whole[:, start : start + count, :].reshape(groups * count, width)

    return take(0, n), take(n, n), take(2 * n, c), take(2 * n + c, c)


def is_last(place):
    return (place[0] == 3) & (place[1] == 3) & (place[2] == 1)


def after(earlier, later, n):
    out = dot32(earlier, later[:n], NN)
    return out[:n], out[n:] + later[n:]


def pair_kernel(place, mine, other, out, beside):
    def own(whole):
        couple0, couple1, source0, source1 = pieces(whole)
        top, bottom = after(
            jnp.concatenate([couple0, source0], axis=0),
            jnp.concatenate([couple1, source1], axis=0),
            couple0.shape[0],
        )
        return jnp.concatenate([top, bottom], axis=0)

    here, there = own(mine), own(other)
    n = here.shape[1]
    upper = place[2] == 1
    first = jnp.where(upper, there, here)
    second = jnp.where(upper, here, there)
    out[:n], out[n:] = after(first, second, n)
    beside[...] = there


def group_kernel(place, mine, one, two, three, total, low, slots):
    n = mine.shape[1]
    y = place[1]
    for d, ref in enumerate((mine, one, two, three)):
        slots[lax.rem(y - d + 4, 4)] = ref[...]

    low_top, low_bottom = after(slots[0], slots[1], n)
    high_top, high_bottom = after(slots[2], slots[3], n)
    low[:n] = low_top
    low[n:] = low_bottom
    out = dot32(low[...], high_top, NN)
    total[:n] = out[:n]
    total[n:] = out[n:] + high_bottom


def tail_kernel(place, whole, other, low, one, maps, shifts, before):
    couple0, _, source0, _ = pieces(whole)
    n = couple0.shape[0]
    y = place[1]
    top, bottom = after(low[...], one, n)
    three = jnp.concatenate([top, bottom], axis=0)
    rows = lax.broadcasted_iota(jnp.int32, low.shape, 0)
    lanes = lax.broadcasted_iota(jnp.int32, low.shape, 1)
    none = jnp.where(rows == lanes, 1.0, 0.0).astype(F32)
    before[...] = jnp.where(
        y == 3, three, jnp.where(y == 2, low[...], jnp.where(y == 1, one[...], none))
    )
    reach, shift = after(before[...], other[...], n)
    upper = place[2] == 1
    reach = jnp.where(upper, reach, before[:n])
    shift = jnp.where(upper, shift, before[n:])
    out = dot32(jnp.concatenate([reach, shift], axis=0), couple0, NN)
    maps[:, :n] = reach
    maps[:, n:] = out[:n]
    shifts[:, :n] = shift
    shifts[:, n:] = out[n:] + source0


def forward_kernel(place, maps, shifts, own, one, two, three, entry, turned, out):
    n = one.shape[1]
    x = place[0]
    state = jnp.where(x == 3, own[n:], 0.0)
    for d, ref in ((3, three), (2, two), (1, one)):
        state = jnp.where(d <= x + 1, dot32(state, ref[:n], NN) + ref[n:], state)
    both = dot32(state, maps[...], NN) + shifts[...]
    states = jnp.concatenate([both[:, :n], both[:, n:]], axis=0)
    high, middle, low = (part.astype(BF16) for part in three_parts(states))
    factor = jnp.concatenate(
        [
            jnp.concatenate([high, low], axis=1),
            jnp.concatenate([middle, jnp.zeros_like(middle)], axis=1),
        ],
        axis=0,
    )
    lanes = lax.broadcasted_iota(jnp.int32, out.shape, 1)
    width = states.shape[0]

    def through(i):
        product = dot16(jnp.concatenate([entry[i], entry[i]], axis=1), factor, NT)
        return product[:, width:] + product[:, :width]

    product = jnp.where(lanes < width // 2, through(0), through(1))
    out[...] = (turned[...] - product).astype(BF16)


def windows(place, blocks, shifts, inverse, padded):
    groups = 8
    local, both = blocks[0].shape
    room = padded.shape[1]
    starts = []
    for k, (block, d) in enumerate(zip(blocks, shifts)):
        owner = lax.rem(place[3] - d + groups, groups)
        odd = lax.rem(owner, 2)
        offset = pl.multiple_of(odd * (room - local), room - local)
        padded[k] = jnp.zeros(padded.shape[1:], BF16)
        padded[k, pl.ds(offset, local), :] = block[...]
        starts.append(pl.multiple_of(owner * local - odd * (room - local), 128))
    whole = padded[...].reshape(len(blocks) * room, both)

    def through(i):
        rows = jnp.concatenate([inverse[i, :, pl.ds(start, room)] for start in starts], axis=1)
        return dot16(rows, whole, NN)

    lanes = lax.broadcasted_iota(jnp.int32, (local, both), 1)
    return jnp.where(lanes < both // 2, through(0), through(1))


EARLY = (0, 1, 2, 4, 6, 7)
LATE = (3, 5)


def early_kernel(place, *refs):
    blocks = refs[: len(EARLY)]
    inverse, out, padded = refs[len(EARLY) :]
    out[...] = windows(place, blocks, EARLY, inverse, padded)


def apply_kernel(place, *refs):
    blocks = refs[: len(LATE)]
    early, inverse, entry, turned, carried, padded = refs[len(LATE) :]
    value = early[...] + windows(place, blocks, LATE, inverse, padded)
    turned[...] = value.T
    low = value.astype(BF16)
    half = value.shape[1] // 2
    c = half // carried.shape[0]
    put(carried, 0, c, dot16(low, entry[0], TN)[:half])
    put(carried, c, c, dot16(low, entry[1], TN)[half:])


def routes_kernel(place, whole, other, before, y1, y2, y3, x1, x2, x3, leave, reach):
    couple0, couple1, _, _ = pieces(whole)
    n = couple0.shape[0]
    rows = lax.broadcasted_iota(jnp.int32, (n, n), 0)
    lanes = lax.broadcasted_iota(jnp.int32, (n, n), 1)
    identity = jnp.where(rows == lanes, 1.0, 0.0).astype(F32)
    x, y, core = place[0], place[1], place[2]
    lower = jnp.where(core == 1, other[:n], identity)
    out = dot32(lower, couple0, NN)
    chip = jnp.concatenate([lower, out], axis=1)
    top = jnp.concatenate([identity, couple0], axis=1)
    store_parts(leave, jnp.concatenate([top, chip, dot32(before[:n], chip, NN)], axis=0))
    here = jnp.where(core == 0, other[:n], identity)
    blocks = [identity]
    for e, ref in ((1, y3), (2, y2), (3, y1)):
        blocks.append(here)
        here = jnp.where(y + e <= 3, dot32(here, ref[:n], NN), here)
    for e, ref in ((1, x3), (2, x2), (3, x1)):
        blocks.append(here)
        if e < 3:
            here = dot32(here, ref[:n], NN)
    stacked = jnp.concatenate(blocks, axis=1)
    store_parts(reach, jnp.concatenate([stacked, dot32(couple1, stacked, NN)], axis=0))


def back_kernel(place, parts, leave, carried, send):
    c = parts.shape[1] // 2
    total = parts[0]
    for k in range(1, parts.shape[0]):
        total = total + parts[k]
    carried[...] = total
    n = total.shape[1]
    x, y = place[0], place[1]
    values = dot_parts(jnp.concatenate([total[:c], total[c:]], axis=1), leave, NT)
    own, chip, group = values[:, :n], values[:, n : 2 * n], values[:, 2 * n :]
    for k in range(send.shape[0]):
        same_x = x == k // 8
        same_y = y == (k // 2) % 4
        send[k] = jnp.where(same_x, jnp.where(same_y, own, chip), group)


def behind_kernel(place, got, carried, reach, out):
    n = carried.shape[1]
    c = carried.shape[0] // 2
    x, y, core = place[0], place[1], place[2]
    terms = [jnp.where(core == 0, got[x * 8 + y * 2 + 1], 0.0)]
    for e in (1, 2, 3):
        base = x * 8 + lax.rem(y + e, 4) * 2
        terms.append(jnp.where(y + e <= 3, got[base] + got[base + 1], 0.0))
    for e in (1, 2, 3):
        base = lax.rem(x + e, 4) * 8
        extra = got[base]
        for k in range(1, 8):
            extra = extra + got[base + k]
        terms.append(jnp.where(x + e <= 3, extra, 0.0))
    values = dot_parts(jnp.concatenate(terms, axis=1), reach, NT)
    state = values[:, :n]
    inner = values[:, n:] + carried[c:]
    for k in range(out.shape[0]):
        out[k, :c] = inner
        out[k, c:] = state


def final_kernel(place, got, turned, exit_, arriving, out):
    groups, rows, width = got.shape
    c = rows // 2
    inner = got[:, :c, :].reshape(groups * c, width)
    outer = got[:, c:, :].reshape(groups * c, width)
    out[0] = turned[: groups * c] - dot32_16(inner, exit_[1], NT)
    out[1] = turned[groups * c :] - dot32_16(outer, arriving[0], NT)


def exchange(value, axes):
    return lax.all_to_all(value, axes, split_axis=0, concat_axis=0, tiled=True)


def ring(value, axis):
    size = lax.axis_size(axis)
    return [
        lax.ppermute(value, axis, [(i, (i + d) % size) for i in range(size)])
        for d in range(1, size)
    ]


def shards(rhs, block_inverse, entry, exit_, previous):
    z = lax.axis_size(COL)
    here, cols, local = rhs.shape
    n = entry.shape[2]
    place = jnp.stack([lax.axis_index(X), lax.axis_index(Y), lax.axis_index(CORE), lax.axis_index(COL)]).astype(jnp.int32)
    chain = lax.axis_size(CHAIN)
    arriving = lax.ppermute(exit_[:1], CHAIN, [(i, (i - 1) % chain) for i in range(chain)])
    rows = (2 * n + 2 * cols) // z
    entry_v, exit_v, second, turned, begun = call(
        load_kernel,
        place,
        [pltpu.with_memory_space_constraint(a, pltpu.HBM) for a in (entry, exit_, rhs, previous)],
        (
            of(entry.shape, BF16),
            of(exit_.shape, BF16),
            of(previous.shape, BF16),
            of((local, 2 * cols)),
            of((z, (n + cols) // z, n)),
        ),
        [
            pltpu.VMEM(rhs.shape, BF16),
            pltpu.VMEM(previous.shape, BF16),
            pltpu.SemaphoreType.DMA((4,)),
        ],
        [hbm()] * 4,
        cost=1 << 28,
    )
    parts = call(partial_kernel, place, (entry_v, arriving, second, begun), of((z, rows, n)))
    summed = call(sum_kernel, place, (exchange(parts, COL),), of((z, rows, n)))
    whole = exchange(summed, COL)
    maps = of((n + cols, n))
    whole_other = lax.ppermute(whole, CORE, [(0, 1), (1, 0)])
    chip, other = call(pair_kernel, place, (whole, whole_other), (maps, maps))
    y1, y2, y3 = ring(chip, Y)
    group, low = call(
        group_kernel, place, (chip, y1, y2, y3), (maps, maps), [pltpu.VMEM((4, n + cols, n), F32)]
    )
    x1, x2, x3 = ring(group, X)
    ahead, shifts, before = call(
        tail_kernel,
        place,
        (whole, other, low, y1),
        (of((n, 2 * n)), of((cols, 2 * n)), maps),
        cost=1 << 27,
    )
    forward = call(
        forward_kernel,
        place,
        (ahead, shifts, group, x1, x2, x3, entry_v, turned),
        of((local, 2 * cols), BF16),
    )
    up = [(i, (i + 1) % z) for i in range(z)]
    down = [(i, (i - 1) % z) for i in range(z)]
    far = [(i, (i + z // 2) % z) for i in range(z)]
    blocks = [forward] + [None] * (z - 1)
    blocks[1] = lax.ppermute(forward, COL, up)
    blocks[7] = lax.ppermute(forward, COL, down)
    blocks[4] = lax.ppermute(forward, COL, far)
    blocks[2] = lax.ppermute(blocks[1], COL, up)
    blocks[6] = lax.ppermute(blocks[7], COL, down)
    leave, reach = call(
        routes_kernel,
        place,
        (whole, other, before, y1, y2, y3, x1, x2, x3),
        (of((3, 3 * n, 2 * n), BF16), of((3, 2 * n, 7 * n), BF16)),
        cost=1 << 29,
    )
    blocks[2], blocks[4], blocks[6], leave, reach = lax.optimization_barrier(
        (blocks[2], blocks[4], blocks[6], leave, reach)
    )
    blocks[3] = lax.ppermute(blocks[2], COL, up)
    blocks[5] = lax.ppermute(blocks[6], COL, down)
    c = cols // z
    room = -(-local // 128) * 128
    early = call(
        early_kernel,
        place,
        (*[blocks[d] for d in EARLY], block_inverse),
        of((local, 2 * cols)),
        [pltpu.VMEM((len(EARLY), room, 2 * cols), BF16)],
        cost=1 << 29,
    )
    turned_applied, carried_parts = call(
        apply_kernel,
        place,
        (*[blocks[d] for d in LATE], early, block_inverse, entry_v),
        (of((2 * cols, local)), of((z, 2 * c, n))),
        [pltpu.VMEM((len(LATE), room, 2 * cols), BF16)],
    )
    carried, send = call(
        back_kernel,
        place,
        (exchange(carried_parts, COL), leave),
        (of((2 * c, n)), of((chain, c, n))),
    )
    behind = call(
        behind_kernel, place, (exchange(send, CHAIN), carried, reach), of((z, 2 * c, n))
    )
    return call(
        final_kernel,
        place,
        (exchange(behind, COL), turned_applied, exit_v, arriving),
        of((here, cols, local)),
    )


def solution(mesh):
    torus = Mesh(mesh.devices.reshape(4, 4, 2, mesh.shape["col"]), (X, Y, CORE, COL))
    return jax.shard_map(
        shards,
        mesh=torus,
        in_specs=(
            P(CHAIN, None, COL),
            P(CHAIN, COL, None),
            P(CHAIN, COL, None),
            P(CHAIN, COL, None),
            P(None, COL),
        ),
        out_specs=P(CHAIN, None, COL),
        check_vma=False,
    )
```

```python
import jax
import jax.numpy as jnp
from jax import lax
from jax.experimental import pallas as pl
from jax.experimental.pallas import tpu as pltpu
from jax.sharding import Mesh
from jax.sharding import PartitionSpec as P

X, Y, CORE, COL = "chain_0", "chain_1", "chain_2", "col"
CHAIN = (X, Y, CORE)
F32 = jnp.float32
BF16 = jnp.bfloat16

NN = (((1,), (0,)), ((), ()))
NT = (((1,), (1,)), ((), ()))
TN = (((0,), (0,)), ((), ()))


def dot16(a, b, dims):
    return lax.dot_general(a, b, dims, preferred_element_type=F32)


def dot32(a, b, dims):
    return dot_parts(a, [part.astype(BF16) for part in three_parts(b)], dims)


def dot32_16(a, b, dims):
    high = a.astype(BF16)
    rest = a - high.astype(F32)
    middle = rest.astype(BF16)
    low = (rest - middle.astype(F32)).astype(BF16)
    rows = a.shape[0]
    out = dot16(jnp.concatenate([high, middle, low], axis=0), b, dims)
    return (out[2 * rows :] + out[rows : 2 * rows]) + out[:rows]


def three_parts(a):
    high = a.astype(BF16).astype(F32)
    middle = (a - high).astype(BF16).astype(F32)
    return high, middle, (a - high) - middle


def store_parts(ref, value):
    for k, part in enumerate(three_parts(value)):
        ref[k] = part.astype(BF16)


def dot_parts(a, b, dims):
    rows = a.shape[0]
    parts = jnp.concatenate(three_parts(a), axis=0)
    by_high = dot16(parts.astype(BF16), b[0], dims)
    by_middle = dot16(parts[: 2 * rows].astype(BF16), b[1], dims)
    by_low = dot16(parts[:rows].astype(BF16), b[2], dims)
    small = (by_low + by_middle[rows:]) + by_high[2 * rows :]
    return (small + (by_middle[:rows] + by_high[rows : 2 * rows])) + by_high[:rows]


def vmem():
    return pl.BlockSpec(memory_space=pltpu.VMEM)


def smem():
    return pl.BlockSpec(memory_space=pltpu.SMEM)


def hbm():
    return pl.BlockSpec(memory_space=pltpu.HBM)


def call(kernel, place, arrays, outs, scratch=(), specs=None, cost=None, room=24):
    return pl.pallas_call(
        kernel,
        out_shape=outs,
        in_specs=[smem()] + (specs or [vmem()] * len(arrays)),
        out_specs=jax.tree.map(lambda _: vmem(), outs),
        scratch_shapes=list(scratch),
        cost_estimate=cost and pl.CostEstimate(flops=cost, bytes_accessed=cost // 100, transcendentals=0),
        compiler_params=pltpu.CompilerParams(vmem_limit_bytes=room * 1024 * 1024),
    )(place, *arrays)


def of(shape, dtype=F32):
    return jax.ShapeDtypeStruct(shape, dtype)


def put(out, start, rows, value):
    groups = out.shape[0]
    out[:, start : start + rows, :] = value.reshape(groups, rows, value.shape[1])


def load_kernel(place, entry, exit_, rhs, previous, entry_v, exit_v, second, turned, out, rhs_v, previous_v, sems):
    copies = [
        pltpu.make_async_copy(source, target, sems.at[i])
        for i, (source, target) in enumerate(
            ((entry, entry_v), (exit_, exit_v), (rhs, rhs_v), (previous, previous_v))
        )
    ]
    for copy in copies:
        copy.start()
    for copy in copies:
        copy.wait()
    groups = out.shape[0]
    n = entry_v.shape[2] // groups
    c = rhs_v.shape[1] // groups
    put(out, 0, n, -dot16(entry_v[0], exit_v[1], TN))
    put(out, n, c, dot16(rhs_v[0], exit_v[1], NN))
    last = is_last(place)
    second[...] = jnp.where(last, previous_v[...].astype(F32), rhs_v[1].astype(F32)).astype(BF16)
    both = jnp.concatenate([rhs_v[0], rhs_v[1]], axis=0).astype(F32)
    turned[...] = both.T


def partial_kernel(place, entry, arriving, second, early, out):
    groups = out.shape[0]
    n = entry.shape[2] // groups
    c = second.shape[0] // groups
    out[:, 0:n, :] = early[:, 0:n, :]
    put(out, n, n, jnp.where(is_last(place), 0.0, -dot16(entry[1], arriving[0], TN)))
    out[:, 2 * n : 2 * n + c, :] = early[:, n : n + c, :]
    put(out, 2 * n + c, c, dot16(second[...], arriving[0], NN))


def sum_kernel(place, parts, out):
    total = parts[0]
    for k in range(1, parts.shape[0]):
        total = total + parts[k]
    for k in range(parts.shape[0]):
        out[k] = total


def pieces(whole):
    groups, rows, width = whole.shape
    n = width // groups
    c = (rows - 2 * n) // 2

    def take(start, count):
        return whole[:, start : start + count, :].reshape(groups * count, width)

    return take(0, n), take(n, n), take(2 * n, c), take(2 * n + c, c)


def is_last(place):
    return (place[0] == 3) & (place[1] == 3) & (place[2] == 1)


def after(earlier, later, n):
    out = dot32(earlier, later[:n], NN)
    return out[:n], out[n:] + later[n:]


def pair_kernel(place, mine, other, out, beside):
    def own(whole):
        couple0, couple1, source0, source1 = pieces(whole)
        top, bottom = after(
            jnp.concatenate([couple0, source0], axis=0),
            jnp.concatenate([couple1, source1], axis=0),
            couple0.shape[0],
        )
        return jnp.concatenate([top, bottom], axis=0)

    here, there = own(mine), own(other)
    n = here.shape[1]
    upper = place[2] == 1
    first = jnp.where(upper, there, here)
    second = jnp.where(upper, here, there)
    out[:n], out[n:] = after(first, second, n)
    beside[...] = there


def group_kernel(place, mine, one, two, three, total, low, slots):
    n = mine.shape[1]
    y = place[1]
    for d, ref in enumerate((mine, one, two, three)):
        slots[lax.rem(y - d + 4, 4)] = ref[...]

    low_top, low_bottom = after(slots[0], slots[1], n)
    high_top, high_bottom = after(slots[2], slots[3], n)
    low[:n] = low_top
    low[n:] = low_bottom
    out = dot32(low[...], high_top, NN)
    total[:n] = out[:n]
    total[n:] = out[n:] + high_bottom


def tail_kernel(place, whole, other, low, one, maps, shifts, before):
    couple0, _, source0, _ = pieces(whole)
    n = couple0.shape[0]
    y = place[1]
    top, bottom = after(low[...], one, n)
    three = jnp.concatenate([top, bottom], axis=0)
    rows = lax.broadcasted_iota(jnp.int32, low.shape, 0)
    lanes = lax.broadcasted_iota(jnp.int32, low.shape, 1)
    none = jnp.where(rows == lanes, 1.0, 0.0).astype(F32)
    before[...] = jnp.where(
        y == 3, three, jnp.where(y == 2, low[...], jnp.where(y == 1, one[...], none))
    )
    reach, shift = after(before[...], other[...], n)
    upper = place[2] == 1
    reach = jnp.where(upper, reach, before[:n])
    shift = jnp.where(upper, shift, before[n:])
    out = dot32(jnp.concatenate([reach, shift], axis=0), couple0, NN)
    maps[:, :n] = reach
    maps[:, n:] = out[:n]
    shifts[:, :n] = shift
    shifts[:, n:] = out[n:] + source0


def forward_kernel(place, maps, shifts, own, one, two, three, entry, turned, out):
    n = one.shape[1]
    x = place[0]
    state = jnp.where(x == 3, own[n:], 0.0)
    for d, ref in ((3, three), (2, two), (1, one)):
        state = jnp.where(d <= x + 1, dot32(state, ref[:n], NN) + ref[n:], state)
    both = dot32(state, maps[...], NN) + shifts[...]
    states = jnp.concatenate([both[:, :n], both[:, n:]], axis=0)
    high, middle, low = (part.astype(BF16) for part in three_parts(states))
    factor = jnp.concatenate(
        [
            jnp.concatenate([high, low], axis=1),
            jnp.concatenate([middle, jnp.zeros_like(middle)], axis=1),
        ],
        axis=0,
    )
    lanes = lax.broadcasted_iota(jnp.int32, out.shape, 1)
    width = states.shape[0]

    def through(i):
        product = dot16(jnp.concatenate([entry[i], entry[i]], axis=1), factor, NT)
        return product[:, width:] + product[:, :width]

    product = jnp.where(lanes < width // 2, through(0), through(1))
    out[...] = (turned[...] - product).astype(BF16)


def windows(place, blocks, shifts, inverse, padded):
    groups = 8
    local, both = blocks[0].shape
    room = padded.shape[1]
    starts = []
    for k, (block, d) in enumerate(zip(blocks, shifts)):
        owner = lax.rem(place[3] - d + groups, groups)
        odd = lax.rem(owner, 2)
        offset = pl.multiple_of(odd * (room - local), room - local)
        padded[k] = jnp.zeros(padded.shape[1:], BF16)
        padded[k, pl.ds(offset, local), :] = block[...]
        starts.append(pl.multiple_of(owner * local - odd * (room - local), 128))
    whole = padded[...].reshape(len(blocks) * room, both)

    def through(i):
        rows = jnp.concatenate([inverse[i, :, pl.ds(start, room)] for start in starts], axis=1)
        return dot16(rows, whole, NN)

    lanes = lax.broadcasted_iota(jnp.int32, (local, both), 1)
    return jnp.where(lanes < both // 2, through(0), through(1))


EARLY = (0, 1, 2, 4, 6, 7)
LATE = (3, 5)


def early_kernel(place, *refs):
    blocks = refs[: len(EARLY)]
    inverse, out, padded = refs[len(EARLY) :]
    out[...] = windows(place, blocks, EARLY, inverse, padded)


def apply_kernel(place, *refs):
    blocks = refs[: len(LATE)]
    early, inverse, entry, leave, turned, send, padded = refs[len(LATE) :]
    value = early[...] + windows(place, blocks, LATE, inverse, padded)
    turned[...] = value.T
    low = value.astype(BF16)
    half = value.shape[1] // 2
    first = dot16(low, entry[0], TN)[:half]
    second = dot16(low, entry[1], TN)[half:]
    n = first.shape[1]
    values = dot_parts(jnp.concatenate([first, second], axis=1), leave, NT)
    own, chip = values[:, :n], values[:, n:]
    c = send.shape[1] // 2
    groups = half // c
    for k in range(send.shape[0]):
        row = (k % groups) * c
        send[k, :c] = chip[row : row + c]
        same = place[2] == k // groups
        send[k, c:] = jnp.where(same, second[row : row + c], own[row : row + c])


def routes_kernel(place, whole, other, y1, y2, y3, x1, x2, x3, leave, reach):
    couple0, couple1, _, _ = pieces(whole)
    n = couple0.shape[0]
    rows = lax.broadcasted_iota(jnp.int32, (n, n), 0)
    lanes = lax.broadcasted_iota(jnp.int32, (n, n), 1)
    identity = jnp.where(rows == lanes, 1.0, 0.0).astype(F32)
    x, y, core = place[0], place[1], place[2]
    lower = jnp.where(core == 1, other[:n], identity)
    out = dot32(lower, couple0, NN)
    chip = jnp.concatenate([lower, out], axis=1)
    top = jnp.concatenate([identity, couple0], axis=1)
    store_parts(leave, jnp.concatenate([top, chip], axis=0))
    here = jnp.where(core == 0, other[:n], identity)
    blocks = [identity]
    for e, ref in ((1, y3), (2, y2), (3, y1)):
        blocks.append(here)
        here = jnp.where(y + e <= 3, dot32(here, ref[:n], NN), here)
    for e, ref in ((1, x3), (2, x2), (3, x1)):
        blocks.append(here)
        if e < 3:
            here = dot32(here, ref[:n], NN)
    stacked = jnp.concatenate(blocks, axis=1)
    store_parts(reach, jnp.concatenate([stacked, dot32(couple1, stacked, NN)], axis=0))


def back_kernel(place, got, before, carried, send):
    c = carried.shape[0] // 2
    n = carried.shape[1]
    groups = got.shape[0] // 2
    core = place[2]

    def summed(base, rows):
        total = got[base, rows]
        for k in range(1, groups):
            total = total + got[base + k, rows]
        return total

    upper, lower = slice(0, c), slice(c, 2 * c)
    chip = summed(0, upper) + summed(groups, upper)
    carried[:c] = summed((1 - core) * groups, lower)
    carried[c:] = summed(core * groups, lower)
    group = dot32(chip, before[:n], NT)
    for k in range(send.shape[0]):
        send[k] = jnp.where(place[0] == k // 4, chip, group)


def behind_kernel(place, got, carried, reach, out):
    n = carried.shape[1]
    c = carried.shape[0] // 2
    x, y, core = place[0], place[1], place[2]
    terms = [jnp.where(core == 0, carried[:c], 0.0)]
    for e in (1, 2, 3):
        terms.append(jnp.where(y + e <= 3, got[x * 4 + lax.rem(y + e, 4)], 0.0))
    for e in (1, 2, 3):
        base = lax.rem(x + e, 4) * 4
        extra = (got[base] + got[base + 1]) + (got[base + 2] + got[base + 3])
        terms.append(jnp.where(x + e <= 3, extra, 0.0))
    values = dot_parts(jnp.concatenate(terms, axis=1), reach, NT)
    state = values[:, :n]
    inner = values[:, n:] + carried[c:]
    for k in range(out.shape[0]):
        out[k, :c] = inner
        out[k, c:] = state


def final_kernel(place, got, turned, exit_, arriving, out):
    groups, rows, width = got.shape
    c = rows // 2
    inner = got[:, :c, :].reshape(groups * c, width)
    outer = got[:, c:, :].reshape(groups * c, width)
    out[0] = turned[: groups * c] - dot32_16(inner, exit_[1], NT)
    out[1] = turned[groups * c :] - dot32_16(outer, arriving[0], NT)


def exchange(value, axes):
    return lax.all_to_all(value, axes, split_axis=0, concat_axis=0, tiled=True)


def ring(value, axis):
    size = lax.axis_size(axis)
    return [
        lax.ppermute(value, axis, [(i, (i + d) % size) for i in range(size)])
        for d in range(1, size)
    ]


def shards(rhs, block_inverse, entry, exit_, previous):
    z = lax.axis_size(COL)
    here, cols, local = rhs.shape
    n = entry.shape[2]
    place = jnp.stack([lax.axis_index(X), lax.axis_index(Y), lax.axis_index(CORE), lax.axis_index(COL)]).astype(jnp.int32)
    chain = lax.axis_size(CHAIN)
    arriving = lax.ppermute(exit_[:1], CHAIN, [(i, (i - 1) % chain) for i in range(chain)])
    rows = (2 * n + 2 * cols) // z
    entry_v, exit_v, second, turned, begun = call(
        load_kernel,
        place,
        [pltpu.with_memory_space_constraint(a, pltpu.HBM) for a in (entry, exit_, rhs, previous)],
        (
            of(entry.shape, BF16),
            of(exit_.shape, BF16),
            of(previous.shape, BF16),
            of((local, 2 * cols)),
            of((z, (n + cols) // z, n)),
        ),
        [
            pltpu.VMEM(rhs.shape, BF16),
            pltpu.VMEM(previous.shape, BF16),
            pltpu.SemaphoreType.DMA((4,)),
        ],
        [hbm()] * 4,
        cost=1 << 28,
    )
    parts = call(partial_kernel, place, (entry_v, arriving, second, begun), of((z, rows, n)))
    summed = call(sum_kernel, place, (exchange(parts, COL),), of((z, rows, n)))
    whole = exchange(summed, COL)
    maps = of((n + cols, n))
    whole_other = lax.ppermute(whole, CORE, [(0, 1), (1, 0)])
    chip, other = call(pair_kernel, place, (whole, whole_other), (maps, maps))
    y1, y2, y3 = ring(chip, Y)
    group, low = call(
        group_kernel, place, (chip, y1, y2, y3), (maps, maps), [pltpu.VMEM((4, n + cols, n), F32)]
    )
    x1, x2, x3 = ring(group, X)
    ahead, shifts, before = call(
        tail_kernel,
        place,
        (whole, other, low, y1),
        (of((n, 2 * n)), of((cols, 2 * n)), maps),
        cost=1 << 27,
    )
    forward = call(
        forward_kernel,
        place,
        (ahead, shifts, group, x1, x2, x3, entry_v, turned),
        of((local, 2 * cols), BF16),
    )
    up = [(i, (i + 1) % z) for i in range(z)]
    down = [(i, (i - 1) % z) for i in range(z)]
    far = [(i, (i + z // 2) % z) for i in range(z)]
    blocks = [forward] + [None] * (z - 1)
    blocks[1] = lax.ppermute(forward, COL, up)
    blocks[7] = lax.ppermute(forward, COL, down)
    blocks[4] = lax.ppermute(forward, COL, far)
    blocks[2] = lax.ppermute(blocks[1], COL, up)
    blocks[6] = lax.ppermute(blocks[7], COL, down)
    leave, reach = call(
        routes_kernel,
        place,
        (whole, other, y1, y2, y3, x1, x2, x3),
        (of((3, 2 * n, 2 * n), BF16), of((3, 2 * n, 7 * n), BF16)),
        cost=1 << 29,
    )
    blocks[2], blocks[4], blocks[6], leave, reach = lax.optimization_barrier(
        (blocks[2], blocks[4], blocks[6], leave, reach)
    )
    blocks[3] = lax.ppermute(blocks[2], COL, up)
    blocks[5] = lax.ppermute(blocks[6], COL, down)
    c = cols // z
    room = -(-local // 128) * 128
    early = call(
        early_kernel,
        place,
        (*[blocks[d] for d in EARLY], block_inverse),
        of((local, 2 * cols)),
        [pltpu.VMEM((len(EARLY), room, 2 * cols), BF16)],
        cost=1 << 29,
    )
    turned_applied, leaving = call(
        apply_kernel,
        place,
        (*[blocks[d] for d in LATE], early, block_inverse, entry_v, leave),
        (of((2 * cols, local)), of((2 * z, 2 * c, n))),
        [pltpu.VMEM((len(LATE), room, 2 * cols), BF16)],
    )
    carried, send = call(
        back_kernel,
        place,
        (exchange(leaving, (CORE, COL)), before),
        (of((2 * c, n)), of((chain // 2, c, n))),
    )
    behind = call(
        behind_kernel, place, (exchange(send, (X, Y)), carried, reach), of((z, 2 * c, n))
    )
    return call(
        final_kernel,
        place,
        (exchange(behind, COL), turned_applied, exit_v, arriving),
        of((here, cols, local)),
    )


def solution(mesh):
    torus = Mesh(mesh.devices.reshape(4, 4, 2, mesh.shape["col"]), (X, Y, CORE, COL))
    return jax.shard_map(
        shards,
        mesh=torus,
        in_specs=(
            P(CHAIN, None, COL),
            P(CHAIN, COL, None),
            P(CHAIN, COL, None),
            P(CHAIN, COL, None),
            P(None, COL),
        ),
        out_specs=P(CHAIN, None, COL),
        check_vma=False,
    )
```

```python
import jax
import jax.numpy as jnp
from jax import lax
from jax.experimental import pallas as pl
from jax.experimental.pallas import tpu as pltpu
from jax.sharding import Mesh
from jax.sharding import PartitionSpec as P

X, Y, CORE, COL = "chain_0", "chain_1", "chain_2", "col"
CHAIN = (X, Y, CORE)
F32 = jnp.float32
BF16 = jnp.bfloat16

NN = (((1,), (0,)), ((), ()))
NT = (((1,), (1,)), ((), ()))
TN = (((0,), (0,)), ((), ()))


def dot16(a, b, dims):
    return lax.dot_general(a, b, dims, preferred_element_type=F32)


def dot32(a, b, dims):
    return dot_parts(a, [part.astype(BF16) for part in three_parts(b)], dims)


def dot32_16(a, b, dims):
    high = a.astype(BF16)
    rest = a - high.astype(F32)
    middle = rest.astype(BF16)
    low = (rest - middle.astype(F32)).astype(BF16)
    rows = a.shape[0]
    out = dot16(jnp.concatenate([high, middle, low], axis=0), b, dims)
    return (out[2 * rows :] + out[rows : 2 * rows]) + out[:rows]


def three_parts(a):
    high = a.astype(BF16).astype(F32)
    middle = (a - high).astype(BF16).astype(F32)
    return high, middle, (a - high) - middle


def store_parts(ref, value):
    for k, part in enumerate(three_parts(value)):
        ref[k] = part.astype(BF16)


def dot_parts(a, b, dims):
    rows = a.shape[0]
    parts = jnp.concatenate(three_parts(a), axis=0)
    by_high = dot16(parts.astype(BF16), b[0], dims)
    by_middle = dot16(parts[: 2 * rows].astype(BF16), b[1], dims)
    by_low = dot16(parts[:rows].astype(BF16), b[2], dims)
    small = (by_low + by_middle[rows:]) + by_high[2 * rows :]
    return (small + (by_middle[:rows] + by_high[rows : 2 * rows])) + by_high[:rows]


def vmem():
    return pl.BlockSpec(memory_space=pltpu.VMEM)


def smem():
    return pl.BlockSpec(memory_space=pltpu.SMEM)


def hbm():
    return pl.BlockSpec(memory_space=pltpu.HBM)


def call(kernel, place, arrays, outs, scratch=(), specs=None, cost=None, room=24):
    return pl.pallas_call(
        kernel,
        out_shape=outs,
        in_specs=[smem()] + (specs or [vmem()] * len(arrays)),
        out_specs=jax.tree.map(lambda _: vmem(), outs),
        scratch_shapes=list(scratch),
        cost_estimate=cost and pl.CostEstimate(flops=cost, bytes_accessed=cost // 100, transcendentals=0),
        compiler_params=pltpu.CompilerParams(vmem_limit_bytes=room * 1024 * 1024),
    )(place, *arrays)


def of(shape, dtype=F32):
    return jax.ShapeDtypeStruct(shape, dtype)


def put(out, start, rows, value):
    groups = out.shape[0]
    out[:, start : start + rows, :] = value.reshape(groups, rows, value.shape[1])


def load_kernel(place, entry, exit_, rhs, previous, entry_v, exit_v, second, turned, out, rhs_v, previous_v, sems):
    copies = [
        pltpu.make_async_copy(source, target, sems.at[i])
        for i, (source, target) in enumerate(
            ((entry, entry_v), (exit_, exit_v), (rhs, rhs_v), (previous, previous_v))
        )
    ]
    for copy in copies:
        copy.start()
    for copy in copies:
        copy.wait()
    groups = out.shape[0]
    n = entry_v.shape[2] // groups
    c = rhs_v.shape[1] // groups
    put(out, 0, n, -dot16(entry_v[0], exit_v[1], TN))
    put(out, n, c, dot16(rhs_v[0], exit_v[1], NN))
    last = is_last(place)
    second[...] = jnp.where(last, previous_v[...].astype(F32), rhs_v[1].astype(F32)).astype(BF16)
    both = jnp.concatenate([rhs_v[0], rhs_v[1]], axis=0).astype(F32)
    turned[...] = both.T


def partial_kernel(place, entry, arriving, second, early, out):
    groups = out.shape[0]
    n = entry.shape[2] // groups
    c = second.shape[0] // groups
    out[:, 0:n, :] = early[:, 0:n, :]
    put(out, n, n, jnp.where(is_last(place), 0.0, -dot16(entry[1], arriving[0], TN)))
    out[:, 2 * n : 2 * n + c, :] = early[:, n : n + c, :]
    put(out, 2 * n + c, c, dot16(second[...], arriving[0], NN))


def sum_kernel(place, parts, out):
    total = parts[0]
    for k in range(1, parts.shape[0]):
        total = total + parts[k]
    for k in range(parts.shape[0]):
        out[k] = total


def pieces(whole):
    groups, rows, width = whole.shape
    n = width // groups
    c = (rows - 2 * n) // 2

    def take(start, count):
        return whole[:, start : start + count, :].reshape(groups * count, width)

    return take(0, n), take(n, n), take(2 * n, c), take(2 * n + c, c)


def is_last(place):
    return (place[0] == 3) & (place[1] == 3) & (place[2] == 1)


def after(earlier, later, n):
    out = dot32(earlier, later[:n], NN)
    return out[:n], out[n:] + later[n:]


def pair_kernel(place, mine, other, out, beside):
    def own(whole):
        couple0, couple1, source0, source1 = pieces(whole)
        top, bottom = after(
            jnp.concatenate([couple0, source0], axis=0),
            jnp.concatenate([couple1, source1], axis=0),
            couple0.shape[0],
        )
        return jnp.concatenate([top, bottom], axis=0)

    here, there = own(mine), own(other)
    n = here.shape[1]
    upper = place[2] == 1
    first = jnp.where(upper, there, here)
    second = jnp.where(upper, here, there)
    out[:n], out[n:] = after(first, second, n)
    beside[...] = there


def group_kernel(place, mine, one, two, three, total, low, slots):
    n = mine.shape[1]
    y = place[1]
    for d, ref in enumerate((mine, one, two, three)):
        slots[lax.rem(y - d + 4, 4)] = ref[...]

    low_top, low_bottom = after(slots[0], slots[1], n)
    high_top, high_bottom = after(slots[2], slots[3], n)
    low[:n] = low_top
    low[n:] = low_bottom
    out = dot32(low[...], high_top, NN)
    total[:n] = out[:n]
    total[n:] = out[n:] + high_bottom


def tail_kernel(place, whole, other, low, one, maps, shifts, before):
    couple0, _, source0, _ = pieces(whole)
    n = couple0.shape[0]
    y = place[1]
    top, bottom = after(low[...], one, n)
    three = jnp.concatenate([top, bottom], axis=0)
    rows = lax.broadcasted_iota(jnp.int32, low.shape, 0)
    lanes = lax.broadcasted_iota(jnp.int32, low.shape, 1)
    none = jnp.where(rows == lanes, 1.0, 0.0).astype(F32)
    before[...] = jnp.where(
        y == 3, three, jnp.where(y == 2, low[...], jnp.where(y == 1, one[...], none))
    )
    reach, shift = after(before[...], other[...], n)
    upper = place[2] == 1
    reach = jnp.where(upper, reach, before[:n])
    shift = jnp.where(upper, shift, before[n:])
    out = dot32(jnp.concatenate([reach, shift], axis=0), couple0, NN)
    maps[:, :n] = reach
    maps[:, n:] = out[:n]
    shifts[:, :n] = shift
    shifts[:, n:] = out[n:] + source0


def forward_kernel(place, maps, shifts, own, one, two, three, entry, turned, out):
    n = one.shape[1]
    x = place[0]
    state = jnp.where(x == 3, own[n:], 0.0)
    for d, ref in ((3, three), (2, two)):
        state = jnp.where(d <= x + 1, dot32(state, ref[:n], NN) + ref[n:], state)
    onward = dot32(one[...], maps[...], NN)
    both = dot32(state, onward[:n], NN) + (onward[n:] + shifts[...])
    states = jnp.concatenate([both[:, :n], both[:, n:]], axis=0)
    high, middle, low = (part.astype(BF16) for part in three_parts(states))
    factor = jnp.concatenate(
        [
            jnp.concatenate([high, low], axis=1),
            jnp.concatenate([middle, jnp.zeros_like(middle)], axis=1),
        ],
        axis=0,
    )
    lanes = lax.broadcasted_iota(jnp.int32, out.shape, 1)
    width = states.shape[0]

    def through(i):
        product = dot16(jnp.concatenate([entry[i], entry[i]], axis=1), factor, NT)
        return product[:, width:] + product[:, :width]

    product = jnp.where(lanes < width // 2, through(0), through(1))
    out[...] = (turned[...] - product).astype(BF16)


def windows(place, blocks, shifts, inverse, padded):
    groups = 8
    local, both = blocks[0].shape
    room = padded.shape[1]
    starts = []
    for k, (block, d) in enumerate(zip(blocks, shifts)):
        owner = lax.rem(place[3] - d + groups, groups)
        odd = lax.rem(owner, 2)
        offset = pl.multiple_of(odd * (room - local), room - local)
        padded[k] = jnp.zeros(padded.shape[1:], BF16)
        padded[k, pl.ds(offset, local), :] = block[...]
        starts.append(pl.multiple_of(owner * local - odd * (room - local), 128))
    whole = padded[...].reshape(len(blocks) * room, both)

    def through(i):
        rows = jnp.concatenate([inverse[i, :, pl.ds(start, room)] for start in starts], axis=1)
        return dot16(rows, whole, NN)

    lanes = lax.broadcasted_iota(jnp.int32, (local, both), 1)
    return jnp.where(lanes < both // 2, through(0), through(1))


EARLY = (0, 1, 2, 4, 6, 7)
LATE = (3, 5)


def early_kernel(place, *refs):
    blocks = refs[: len(EARLY)]
    inverse, out, padded = refs[len(EARLY) :]
    out[...] = windows(place, blocks, EARLY, inverse, padded)


def apply_kernel(place, *refs):
    blocks = refs[: len(LATE)]
    early, inverse, entry, turned, carried, padded = refs[len(LATE) :]
    value = early[...] + windows(place, blocks, LATE, inverse, padded)
    turned[...] = value.T
    low = value.astype(BF16)
    half = value.shape[1] // 2
    c = half // carried.shape[0]
    put(carried, 0, c, dot16(low, entry[0], TN)[:half])
    put(carried, c, c, dot16(low, entry[1], TN)[half:])


def routes_kernel(place, whole, other, before, y1, y2, y3, x1, x2, x3, leave, reach):
    couple0, couple1, _, _ = pieces(whole)
    n = couple0.shape[0]
    rows = lax.broadcasted_iota(jnp.int32, (n, n), 0)
    lanes = lax.broadcasted_iota(jnp.int32, (n, n), 1)
    identity = jnp.where(rows == lanes, 1.0, 0.0).astype(F32)
    x, y, core = place[0], place[1], place[2]
    lower = jnp.where(core == 1, other[:n], identity)
    out = dot32(lower, couple0, NN)
    chip = jnp.concatenate([lower, out], axis=1)
    top = jnp.concatenate([identity, couple0], axis=1)
    store_parts(leave, jnp.concatenate([top, chip, dot32(before[:n], chip, NN)], axis=0))
    here = jnp.where(core == 0, other[:n], identity)
    blocks = [identity]
    for e, ref in ((1, y3), (2, y2), (3, y1)):
        blocks.append(here)
        here = jnp.where(y + e <= 3, dot32(here, ref[:n], NN), here)
    for e, ref in ((1, x3), (2, x2), (3, x1)):
        blocks.append(here)
        if e < 3:
            here = dot32(here, ref[:n], NN)
    stacked = jnp.concatenate(blocks, axis=1)
    store_parts(reach, jnp.concatenate([stacked, dot32(couple1, stacked, NN)], axis=0))


def back_kernel(place, parts, leave, carried, send):
    c = parts.shape[1] // 2
    total = parts[0]
    for k in range(1, parts.shape[0]):
        total = total + parts[k]
    carried[...] = total
    n = total.shape[1]
    x, y = place[0], place[1]
    values = dot_parts(jnp.concatenate([total[:c], total[c:]], axis=1), leave, NT)
    own, chip, group = values[:, :n], values[:, n : 2 * n], values[:, 2 * n :]
    for k in range(send.shape[0]):
        same_x = x == k // 8
        same_y = y == (k // 2) % 4
        send[k] = jnp.where(same_x, jnp.where(same_y, own, chip), group)


def behind_kernel(place, got, carried, reach, out):
    n = carried.shape[1]
    c = carried.shape[0] // 2
    x, y, core = place[0], place[1], place[2]
    terms = [jnp.where(core == 0, got[x * 8 + y * 2 + 1], 0.0)]
    for e in (1, 2, 3):
        base = x * 8 + lax.rem(y + e, 4) * 2
        terms.append(jnp.where(y + e <= 3, got[base] + got[base + 1], 0.0))
    for e in (1, 2, 3):
        base = lax.rem(x + e, 4) * 8
        extra = got[base]
        for k in range(1, 8):
            extra = extra + got[base + k]
        terms.append(jnp.where(x + e <= 3, extra, 0.0))
    values = dot_parts(jnp.concatenate(terms, axis=1), reach, NT)
    state = values[:, :n]
    inner = values[:, n:] + carried[c:]
    for k in range(out.shape[0]):
        out[k, :c] = inner
        out[k, c:] = state


def final_kernel(place, got, turned, exit_, arriving, out):
    groups, rows, width = got.shape
    c = rows // 2
    inner = got[:, :c, :].reshape(groups * c, width)
    outer = got[:, c:, :].reshape(groups * c, width)
    out[0] = turned[: groups * c] - dot32_16(inner, exit_[1], NT)
    out[1] = turned[groups * c :] - dot32_16(outer, arriving[0], NT)


def exchange(value, axes):
    return lax.all_to_all(value, axes, split_axis=0, concat_axis=0, tiled=True)


def ring(value, axis):
    size = lax.axis_size(axis)
    return [
        lax.ppermute(value, axis, [(i, (i + d) % size) for i in range(size)])
        for d in range(1, size)
    ]


def shards(rhs, block_inverse, entry, exit_, previous):
    z = lax.axis_size(COL)
    here, cols, local = rhs.shape
    n = entry.shape[2]
    place = jnp.stack([lax.axis_index(X), lax.axis_index(Y), lax.axis_index(CORE), lax.axis_index(COL)]).astype(jnp.int32)
    chain = lax.axis_size(CHAIN)
    arriving = lax.ppermute(exit_[:1], CHAIN, [(i, (i - 1) % chain) for i in range(chain)])
    rows = (2 * n + 2 * cols) // z
    entry_v, exit_v, second, turned, begun = call(
        load_kernel,
        place,
        [pltpu.with_memory_space_constraint(a, pltpu.HBM) for a in (entry, exit_, rhs, previous)],
        (
            of(entry.shape, BF16),
            of(exit_.shape, BF16),
            of(previous.shape, BF16),
            of((local, 2 * cols)),
            of((z, (n + cols) // z, n)),
        ),
        [
            pltpu.VMEM(rhs.shape, BF16),
            pltpu.VMEM(previous.shape, BF16),
            pltpu.SemaphoreType.DMA((4,)),
        ],
        [hbm()] * 4,
        cost=1 << 28,
    )
    parts = call(partial_kernel, place, (entry_v, arriving, second, begun), of((z, rows, n)))
    summed = call(sum_kernel, place, (exchange(parts, COL),), of((z, rows, n)))
    whole = exchange(summed, COL)
    maps = of((n + cols, n))
    whole_other = lax.ppermute(whole, CORE, [(0, 1), (1, 0)])
    chip, other = call(pair_kernel, place, (whole, whole_other), (maps, maps))
    y1, y2, y3 = ring(chip, Y)
    group, low = call(
        group_kernel, place, (chip, y1, y2, y3), (maps, maps), [pltpu.VMEM((4, n + cols, n), F32)]
    )
    x1, x2, x3 = ring(group, X)
    ahead, shifts, before = call(
        tail_kernel,
        place,
        (whole, other, low, y1),
        (of((n, 2 * n)), of((cols, 2 * n)), maps),
        cost=1 << 27,
    )
    forward = call(
        forward_kernel,
        place,
        (ahead, shifts, group, x1, x2, x3, entry_v, turned),
        of((local, 2 * cols), BF16),
    )
    up = [(i, (i + 1) % z) for i in range(z)]
    down = [(i, (i - 1) % z) for i in range(z)]
    far = [(i, (i + z // 2) % z) for i in range(z)]
    blocks = [forward] + [None] * (z - 1)
    blocks[1] = lax.ppermute(forward, COL, up)
    blocks[7] = lax.ppermute(forward, COL, down)
    blocks[4] = lax.ppermute(forward, COL, far)
    blocks[2] = lax.ppermute(blocks[1], COL, up)
    blocks[6] = lax.ppermute(blocks[7], COL, down)
    leave, reach = call(
        routes_kernel,
        place,
        (whole, other, before, y1, y2, y3, x1, x2, x3),
        (of((3, 3 * n, 2 * n), BF16), of((3, 2 * n, 7 * n), BF16)),
        cost=1 << 29,
    )
    blocks[2], blocks[4], blocks[6], leave, reach = lax.optimization_barrier(
        (blocks[2], blocks[4], blocks[6], leave, reach)
    )
    blocks[3] = lax.ppermute(blocks[2], COL, up)
    blocks[5] = lax.ppermute(blocks[6], COL, down)
    c = cols // z
    room = -(-local // 128) * 128
    early = call(
        early_kernel,
        place,
        (*[blocks[d] for d in EARLY], block_inverse),
        of((local, 2 * cols)),
        [pltpu.VMEM((len(EARLY), room, 2 * cols), BF16)],
        cost=1 << 29,
    )
    turned_applied, carried_parts = call(
        apply_kernel,
        place,
        (*[blocks[d] for d in LATE], early, block_inverse, entry_v),
        (of((2 * cols, local)), of((z, 2 * c, n))),
        [pltpu.VMEM((len(LATE), room, 2 * cols), BF16)],
    )
    carried, send = call(
        back_kernel,
        place,
        (exchange(carried_parts, COL), leave),
        (of((2 * c, n)), of((chain, c, n))),
    )
    behind = call(
        behind_kernel, place, (exchange(send, CHAIN), carried, reach), of((z, 2 * c, n))
    )
    return call(
        final_kernel,
        place,
        (exchange(behind, COL), turned_applied, exit_v, arriving),
        of((here, cols, local)),
    )


def solution(mesh):
    torus = Mesh(mesh.devices.reshape(4, 4, 2, mesh.shape["col"]), (X, Y, CORE, COL))
    return jax.shard_map(
        shards,
        mesh=torus,
        in_specs=(
            P(CHAIN, None, COL),
            P(CHAIN, COL, None),
            P(CHAIN, COL, None),
            P(CHAIN, COL, None),
            P(None, COL),
        ),
        out_specs=P(CHAIN, None, COL),
        check_vma=False,
    )
```
